32 devices in a mesh: clip: 8 (over z, x), seq: 4 (over y, core).
Axes of the slice: x: 2, y: 2, z: 4, core: 2. Of those that a mesh axis runs over, the one named last changes fastest.
Arguments:
- clips: bfloat16 [8, 512, 512], P('clip', 'seq'), may hold values from -6 to 6
- lengths: int32 [8], P('clip'), may hold values from 128 to 512
- ff_in: bfloat16 [2, 512, 2048], P(None, 'clip'), may hold values from -0.25 to 0.25
- ff_in_bias: bfloat16 [2, 2048], P(None, 'clip'), may hold values from -3 to 3
- ff_out: bfloat16 [2, 2048, 512], P(None, 'clip'), may hold values from -0.25 to 0.25
- ff_out_bias: bfloat16 [2, 512], P(None, 'clip'), may hold values from -3 to 3
- attn_in: bfloat16 [3, 512, 512], P(None, 'clip'), may hold values from -0.25 to 0.25
- attn_out: bfloat16 [512, 512], P('clip'), may hold values from -1 to 1
- conv_in: bfloat16 [512, 1024], P('clip'), may hold values from -0.25 to 0.25
- conv_depth: bfloat16 [31, 512], P(None, 'clip'), may hold values from -1 to 1
- conv_out: bfloat16 [512, 512], P('clip'), may hold values from -0.25 to 0.25
- bn_affine: bfloat16 [2, 512], P(None, 'clip'), may hold values from 0.5 to 1.5
- norm_gain: bfloat16 [5, 512], P(None, 'clip'), may hold values from 0.5 to 1.5
- norm_bias: bfloat16 [5, 512], P(None, 'clip'), may hold values from -0.5 to 0.5
- slope: float32 [8], replicated, may hold values from 0.05 to 2
- out_grad: bfloat16 [8, 512, 512], P('clip', 'seq'), may hold values from -6 to 6
Outputs:
- out: bfloat16 [8, 512, 512], P('clip', 'seq')
- clips_grad: float32 [8, 512, 512], P('clip', 'seq')
- ff_in_grad: float32 [2, 512, 2048], P(None, 'clip')
- ff_in_bias_grad: float32 [2, 2048], P(None, 'clip')
- ff_out_grad: float32 [2, 2048, 512], P(None, 'clip')
- ff_out_bias_grad: float32 [2, 512], P(None, 'clip')
- attn_in_grad: float32 [3, 512, 512], P(None, 'clip')
- attn_out_grad: float32 [512, 512], P('clip')
- conv_in_grad: float32 [512, 1024], P('clip')
- conv_depth_grad: float32 [31, 512], P(None, 'clip')
- conv_out_grad: float32 [512, 512], P('clip')
- bn_affine_grad: float32 [2, 512], P(None, 'clip')
- norm_gain_grad: float32 [5, 512], P(None, 'clip')
- norm_bias_grad: float32 [5, 512], P(None, 'clip')
- slope_grad: float32 [8], replicated
The draws below stay inside these ranges and needn't reach their ends.
Inputs may be any that keep to these rules, and one draw needn't show every extreme that they name: lengths[c] is the number of valid tokens of clip c; tokens from it on are padding.
All inputs are finite; a program needn't handle non-finite values.
Results may differ from the reference program's by a relative error of at most 0.024.
Values may be sent and summed in bfloat16 or wider, within the bound.
No kernel may reach another device: no remote copies, remote signals or barrier semaphores. Data moves between devices by JAX's collectives and lax.ppermute only.
A program may use at most 128 MiB of HBM per device.

```python
import math
import jax
import jax.numpy as jnp
from jax import lax

D = 512
FF = 2048
HEADS = 8
KERNEL = 31
LENGTH = 512
CLIPS = 8


def place_ends(drawn, rng, smallest, high):
    shape = drawn.shape
    spot = [jax.random.randint(jax.random.fold_in(rng, axis), (), 0, shape[axis]) for axis in range(len(shape))]
    drawn = drawn.at[tuple(spot)].set(smallest)
    longest = shape.index(max(shape))
    spot[longest] = (spot[longest] + 1) % shape[longest]
    return drawn.at[tuple(spot)].set(high)


def steps_of(own_key, shape, split, low, top_value):
    factor_of = 1.0
    for axis_at, shards_of in split:
        draws = jax.random.uniform(jax.random.fold_in(jax.random.fold_in(own_key, 6), axis_at), (shards_of,), jnp.float32, low / len(split), top_value / len(split))
        factor_of = factor_of * jnp.repeat(jnp.exp(draws), shape[axis_at] // shards_of).reshape((-1,) + (1,) * (len(shape) - 1 - axis_at))
    return factor_of


def noise(rng, extent, deviation, limit, cuts=(), dtype=jnp.bfloat16):
    values = deviation * jax.random.normal(rng, extent, jnp.float32)
    if cuts:
        values = values * steps_of(rng, extent, cuts, -0.22, 0.18)
    return jnp.clip(values, -limit, limit).astype(dtype)


def setup_inputs(seed: int = 0) -> dict:
    streams_of = jax.random.split(jax.random.key(seed), 17)
    return {
        "clips": noise(streams_of[0], (CLIPS, LENGTH, D), 1.0, 6.0, ((0, 8), (1, 4))),
        "lengths": place_ends(jax.random.randint(streams_of[1], (CLIPS,), LENGTH // 4, LENGTH + 1), jax.random.fold_in(streams_of[1], 1), LENGTH // 4, LENGTH).astype(jnp.int32),
        "ff_in": noise(streams_of[2], (2, D, FF), D ** -0.5, 0.25, ((1, 8),)),
        "ff_in_bias": noise(streams_of[3], (2, FF), 0.5, 3.0, ((1, 8),)),
        "ff_out": noise(streams_of[4], (2, FF, D), (FF // 4) ** -0.5, 0.25, ((1, 8),)),
        "ff_out_bias": noise(streams_of[5], (2, D), 0.5, 3.0, ((1, 8),)),
        "attn_in": noise(streams_of[6], (3, D, D), D ** -0.5, 0.25, ((1, 8),)),
        "attn_out": noise(streams_of[7], (D, D), (D // 16) ** -0.5, 1.0, ((0, 8),)),
        "conv_in": noise(streams_of[8], (D, 2 * D), D ** -0.5, 0.25, ((0, 8),)),
        "conv_depth": noise(streams_of[9], (KERNEL, D), KERNEL ** -0.5, 1.0, ((1, 8),)),
        "conv_out": noise(streams_of[10], (D, D), D ** -0.5, 0.25, ((0, 8),)),
        "bn_affine": jnp.clip(0.5 + 1.0 * jax.random.uniform(streams_of[11], (2, D), jnp.float32) ** steps_of(streams_of[11], (2, D), ((1, 8),), -0.2, 0.2), 0.5, 1.5).astype(jnp.bfloat16),
        "norm_gain": jnp.clip(1.0 + 0.1 * jax.random.normal(streams_of[12], (5, D), jnp.float32), 0.5, 1.5).astype(jnp.bfloat16),
        "norm_bias": jnp.clip(jax.random.uniform(streams_of[13], (5, D), jnp.float32, -0.5, 0.5) * steps_of(streams_of[13], (5, D), ((1, 8),), -0.4, 0.0), -0.5, 0.5).astype(jnp.bfloat16),
        "slope": jnp.clip(jnp.exp(jax.random.uniform(streams_of[14], (HEADS,), jnp.float32, math.log(0.05), math.log(2.0))), 0.05, 2.0),
        "out_grad": noise(streams_of[15], (CLIPS, LENGTH, D), 1.0, 6.0, ((0, 8), (1, 4))),
    }


NORM_EPS = 1e-05
SCORE_SCALE = 0.125

def swish(values):
    return values * jax.nn.sigmoid(values)

def swish_slope(values):
    sigmoid_v = jax.nn.sigmoid(values)
    return sigmoid_v * (1.0 + values * (1.0 - sigmoid_v))

def norm_forward(resid, gain, shift):
    average = lax.optimization_barrier(jnp.mean(resid, axis=-1, keepdims=True))
    centred = resid - average
    variance = lax.optimization_barrier(jnp.mean(centred * centred, axis=-1, keepdims=True))
    inv_std = lax.rsqrt(variance + NORM_EPS)
    normed = centred * inv_std
    return (normed * gain + shift, normed, inv_std)

def norm_backward(cotangent, normed, inv_std, gain):
    scaled = cotangent * gain
    inner_sum = scaled - lax.optimization_barrier(jnp.mean(scaled, axis=-1, keepdims=True)) - normed * lax.optimization_barrier(jnp.mean(scaled * normed, axis=-1, keepdims=True))
    return (inv_std * inner_sum, lax.optimization_barrier(jnp.sum(cotangent * normed, axis=0)), lax.optimization_barrier(jnp.sum(cotangent, axis=0)))

def feed_forward(resid, gain, shift, w_in, b_in, w_out, b_out):
    normed_out, normed, inv_std = norm_forward(resid, gain, shift)
    act_in = normed_out.astype(jnp.bfloat16)
    before = jnp.dot(act_in, w_in, preferred_element_type=jnp.float32) + b_in
    hidden = swish(before).astype(jnp.bfloat16)
    result = jnp.dot(hidden, w_out, preferred_element_type=jnp.float32) + b_out
    return (resid + 0.5 * result, (act_in, normed, inv_std, before, hidden))

def feed_backward(cotangent, kept_vals, gain, w_in, w_out):
    act_in, normed, inv_std, before, hidden = kept_vals
    halved = 0.5 * cotangent
    halved_b = halved.astype(jnp.bfloat16)
    grad_wout = jnp.dot(hidden.T, halved_b, preferred_element_type=jnp.float32)
    grad_bout = lax.optimization_barrier(jnp.sum(halved, axis=0))
    grad_hidden = jnp.dot(halved_b, w_out.T, preferred_element_type=jnp.float32)
    grad_before = grad_hidden * swish_slope(before)
    grad_before_b = grad_before.astype(jnp.bfloat16)
    grad_win = jnp.dot(act_in.T, grad_before_b, preferred_element_type=jnp.float32)
    grad_bin = lax.optimization_barrier(jnp.sum(grad_before, axis=0))
    grad_act = jnp.dot(grad_before_b, w_in.T, preferred_element_type=jnp.float32)
    grad_res, grad_gain, grad_shift = norm_backward(grad_act, normed, inv_std, gain)
    return (cotangent + grad_res, (grad_win, grad_bin, grad_wout, grad_bout, grad_gain, grad_shift))

def depth_conv(padded, depth, row_count):
    accum = jnp.zeros((row_count, padded.shape[1]), jnp.float32)
    for kernel_tap in range(depth.shape[0]):
        accum = accum + depth[kernel_tap] * padded[kernel_tap:kernel_tap + row_count].astype(jnp.float32)
    return accum

def depth_back(grad_padded, grad_local, padded, depth):
    taps = depth.shape[0]
    row_count = grad_local.shape[0]
    local_f = grad_local.astype(jnp.float32)
    grad_in = jnp.zeros((row_count, padded.shape[1]), jnp.float32)
    tap_grads = []
    for kernel_tap in range(taps):
        lower = taps - 1 - kernel_tap
        grad_in = grad_in + depth[kernel_tap] * grad_padded[lower:lower + row_count].astype(jnp.float32)
        tap_grads.append(lax.optimization_barrier(jnp.sum(local_f * padded[kernel_tap:kernel_tap + row_count].astype(jnp.float32), axis=0)))
    return (grad_in, jnp.stack(tap_grads))

def conv_front(resid, gain, shift, weight_in, depth, token_mask):
    normed_out, normed, inv_std = norm_forward(resid, gain, shift)
    conv_input = normed_out.astype(jnp.bfloat16)
    mixed = jnp.dot(conv_input, weight_in, preferred_element_type=jnp.float32)
    half_cols = mixed.shape[1] // 2
    linear = mixed[:, :half_cols]
    gate_open = jax.nn.sigmoid(mixed[:, half_cols:])
    gated = (token_mask * linear * gate_open).astype(jnp.bfloat16)
    padded = jnp.pad(gated, ((KERNEL // 2, KERNEL // 2), (0, 0)))
    convolved = depth_conv(padded, depth, resid.shape[0])
    return (convolved, (conv_input, normed, inv_std, linear, gate_open, padded))

def head_scores(q_block, key_h, offset, slope_h, length):
    key_pos = jnp.arange(key_h.shape[0]).astype(jnp.int32)
    row_pos = offset + jnp.arange(q_block.shape[0]).astype(jnp.int32)
    distance = jnp.log1p(jnp.abs(row_pos[:, None] - key_pos[None, :]).astype(jnp.float32))
    raw_scores = jnp.dot(q_block, key_h.T, preferred_element_type=jnp.float32) * SCORE_SCALE
    scores = jnp.where((key_pos < length)[None, :], raw_scores - slope_h * distance, -jnp.inf)
    return (scores, distance)

def head_forward(query_h, key_h, value_h, slope_h, length):
    key_count = query_h.shape[0]
    block_rows = min(512, key_count)
    offsets = (jnp.arange(key_count // block_rows) * block_rows).astype(jnp.int32)

    def one_block(offset):
        q_block = lax.dynamic_slice_in_dim(query_h, offset, block_rows, 0)
        scores, _ = head_scores(q_block, key_h, offset, slope_h, length)
        highest = lax.optimization_barrier(jnp.max(scores, axis=-1, keepdims=True))
        log_total = highest + jnp.log(lax.optimization_barrier(jnp.sum(jnp.exp(scores - highest), axis=-1, keepdims=True)))
        attn_probs = jnp.exp(scores - log_total).astype(jnp.bfloat16)
        result = jnp.dot(attn_probs, value_h, preferred_element_type=jnp.float32)
        return (result.astype(jnp.bfloat16), log_total[:, 0])
    outputs, log_totals = lax.map(one_block, offsets)
    return (outputs.reshape(key_count, -1), log_totals.reshape(key_count))

def head_backward(query_h, key_h, value_h, slope_h, length, log_totals, grad_out):
    key_count = query_h.shape[0]
    block_rows = min(512, key_count)
    offsets = (jnp.arange(key_count // block_rows) * block_rows).astype(jnp.int32)

    def one_block(running, inputs_now):
        grad_key, grad_value, grad_slope = running
        offset, log_block = inputs_now
        q_block = lax.dynamic_slice_in_dim(query_h, offset, block_rows, 0)
        grad_rows = lax.dynamic_slice_in_dim(grad_out, offset, block_rows, 0)
        scores, distance = head_scores(q_block, key_h, offset, slope_h, length)
        attn_probs = jnp.exp(scores - log_block[:, None])
        grad_probs = jnp.dot(grad_rows, value_h.T, preferred_element_type=jnp.float32)
        inner_sum = lax.optimization_barrier(jnp.sum(attn_probs * grad_probs, axis=-1, keepdims=True))
        grad_scores = attn_probs * (grad_probs - inner_sum)
        grad_slope = grad_slope - jnp.sum(grad_scores * distance)
        grad_scores_b = grad_scores.astype(jnp.bfloat16)
        grad_query = SCORE_SCALE * jnp.dot(grad_scores_b, key_h, preferred_element_type=jnp.float32)
        grad_key = grad_key + SCORE_SCALE * jnp.dot(grad_scores_b.T, q_block, preferred_element_type=jnp.float32)
        grad_value = grad_value + jnp.dot(attn_probs.astype(jnp.bfloat16).T, grad_rows, preferred_element_type=jnp.float32)
        return ((grad_key, grad_value, grad_slope), grad_query)
    empty = jnp.zeros(key_h.shape, jnp.float32)
    (grad_key, grad_value, grad_slope), grad_query = lax.scan(one_block, (empty, empty, jnp.zeros((), jnp.float32)), (offsets, log_totals.reshape(-1, block_rows)))
    return (grad_query.reshape(key_count, -1).astype(jnp.bfloat16), grad_key.astype(jnp.bfloat16), grad_value.astype(jnp.bfloat16), grad_slope)

def split_heads(matrix):
    return matrix.reshape(matrix.shape[0], HEADS, -1).transpose(1, 0, 2)

def join_heads(stacked):
    return stacked.transpose(1, 0, 2).reshape(stacked.shape[1], -1)

def attention_forward(resid, gain, shift, weights_in, weight_out, slope, length):
    normed_out, normed, inv_std = norm_forward(resid, gain, shift)
    att_in = normed_out.astype(jnp.bfloat16)
    query = jnp.dot(att_in, weights_in[0], preferred_element_type=jnp.float32).astype(jnp.bfloat16)
    key_tok = jnp.dot(att_in, weights_in[1], preferred_element_type=jnp.float32).astype(jnp.bfloat16)
    value_tok = jnp.dot(att_in, weights_in[2], preferred_element_type=jnp.float32).astype(jnp.bfloat16)

    def per_head(inputs_now):
        query_h, key_h, value_h, slope_h = inputs_now
        return head_forward(query_h, key_h, value_h, slope_h, length)
    outputs, log_totals = lax.map(per_head, (split_heads(query), split_heads(key_tok), split_heads(value_tok), slope))
    att_out = join_heads(outputs)
    resid_next = resid + jnp.dot(att_out, weight_out, preferred_element_type=jnp.float32)
    return (resid_next, (att_in, normed, inv_std, query, key_tok, value_tok, att_out, log_totals))

def attention_backward(cotangent, kept_vals, gain, weights_in, weight_out, slope, length):
    att_in, normed, inv_std, query, key_tok, value_tok, att_out, log_totals = kept_vals
    cot_b = cotangent.astype(jnp.bfloat16)
    grad_wout = jnp.dot(att_out.T, cot_b, preferred_element_type=jnp.float32)
    grad_att = jnp.dot(cot_b, weight_out.T, preferred_element_type=jnp.float32).astype(jnp.bfloat16)

    def per_head(inputs_now):
        query_h, key_h, value_h, slope_h, log_h, grad_h = inputs_now
        return head_backward(query_h, key_h, value_h, slope_h, length, log_h, grad_h)
    grad_query, grad_key, grad_value, grad_slope = lax.map(per_head, (split_heads(query), split_heads(key_tok), split_heads(value_tok), slope, log_totals, split_heads(grad_att)))
    head_grads = (join_heads(grad_query), join_heads(grad_key), join_heads(grad_value))
    grad_win = jnp.stack([jnp.dot(att_in.T, piece, preferred_element_type=jnp.float32) for piece in head_grads])
    grad_act = jnp.dot(head_grads[0], weights_in[0].T, preferred_element_type=jnp.float32)
    grad_act = grad_act + jnp.dot(head_grads[1], weights_in[1].T, preferred_element_type=jnp.float32)
    grad_act = grad_act + jnp.dot(head_grads[2], weights_in[2].T, preferred_element_type=jnp.float32)
    grad_res, grad_gain, grad_shift = norm_backward(grad_act, normed, inv_std, gain)
    return (cotangent + grad_res, (grad_win, grad_wout, grad_gain, grad_shift, grad_slope))

def reference(clips, lengths, ff_in, ff_in_bias, ff_out, ff_out_bias, attn_in, attn_out, conv_in, conv_depth, conv_out, bn_affine, norm_gain, norm_bias, slope, out_grad):
    norm_gains = norm_gain.astype(jnp.float32)
    shifts = norm_bias.astype(jnp.float32)
    bias_in = ff_in_bias.astype(jnp.float32)
    bias_out = ff_out_bias.astype(jnp.float32)
    depth = conv_depth.astype(jnp.float32)
    affine = bn_affine.astype(jnp.float32)
    positions = jnp.arange(LENGTH).astype(jnp.int32)

    def front(running, inputs_now):
        clip_rows, length = inputs_now
        token_mask = (positions < length).astype(jnp.float32)[:, None]
        resid0 = clip_rows.astype(jnp.float32)
        resid1, _ = feed_forward(resid0, norm_gains[0], shifts[0], ff_in[0], bias_in[0], ff_out[0], bias_out[0])
        resid2, _ = attention_forward(resid1, norm_gains[1], shifts[1], attn_in, attn_out, slope, length)
        convolved, _ = conv_front(resid2, norm_gains[2], shifts[2], conv_in, depth, token_mask)
        sums_now = (running[0] + lax.optimization_barrier(jnp.sum(token_mask * convolved, axis=0)), running[1] + lax.optimization_barrier(jnp.sum(token_mask * convolved * convolved, axis=0)))
        return (sums_now, (resid1, resid2, convolved))
    zero_row = jnp.zeros((D,), jnp.float32)
    (sum_one, sum_two), (resids1, resids2, convs) = lax.scan(front, (zero_row, zero_row), (clips, lengths))
    valid_count = jnp.sum(lengths).astype(jnp.float32)
    average = sum_one / valid_count
    variance = sum_two / valid_count - average * average
    batch_inv = lax.rsqrt(variance + NORM_EPS)

    def middle(running, inputs_now):
        resid2, convolved, cotangent = inputs_now
        centred = convolved - average
        bnormed = centred * batch_inv
        batch_out = bnormed * affine[0] + affine[1]
        activ = swish(batch_out).astype(jnp.bfloat16)
        resid3 = resid2 + jnp.dot(activ, conv_out, preferred_element_type=jnp.float32)
        resid4, ff_kept = feed_forward(resid3, norm_gains[3], shifts[3], ff_in[1], bias_in[1], ff_out[1], bias_out[1])
        final, final_normed, final_inv = norm_forward(resid4, norm_gains[4], shifts[4])
        grad4, gain_four, shift_four = norm_backward(cotangent.astype(jnp.float32), final_normed, final_inv, norm_gains[4])
        grad3, ff_grads = feed_backward(grad4, ff_kept, norm_gains[3], ff_in[1], ff_out[1])
        grad3_b = grad3.astype(jnp.bfloat16)
        grad_convout = jnp.dot(activ.T, grad3_b, preferred_element_type=jnp.float32)
        grad_batch = jnp.dot(grad3_b, conv_out.T, preferred_element_type=jnp.float32) * swish_slope(batch_out)
        grad_affine = jnp.stack([lax.optimization_barrier(jnp.sum(grad_batch * bnormed, axis=0)), lax.optimization_barrier(jnp.sum(grad_batch, axis=0))])
        grad_centred = grad_batch * affine[0]
        sums_now = (running[0] + lax.optimization_barrier(jnp.sum(grad_centred, axis=0)), running[1] + lax.optimization_barrier(jnp.sum(grad_centred * centred, axis=0)))
        return (sums_now, (final.astype(jnp.bfloat16), grad3, grad_centred, ff_grads, gain_four, shift_four, grad_convout, grad_affine))
    (sum_a, sum_b), middle_out = lax.scan(middle, (zero_row, zero_row), (resids2, convs, out_grad))
    finals, grads3, grad_centreds, ff2_grads, gain_fours, shift_fours, convout_grads, affine_grads = middle_out
    grad_var = -0.5 * batch_inv ** 3 * sum_b
    grad_avg = -batch_inv * sum_a - 2.0 * average * grad_var

    def back(running, inputs_now):
        clip_rows, length, resid1, resid2, convolved, grad3, grad_centred = inputs_now
        token_mask = (positions < length).astype(jnp.float32)[:, None]
        resid0 = clip_rows.astype(jnp.float32)
        _, conv_kept = conv_front(resid2, norm_gains[2], shifts[2], conv_in, depth, token_mask)
        conv_input, normed, inv_std, linear, gate_open, padded = conv_kept
        grad_conv = (grad_centred * batch_inv + token_mask * (grad_avg + 2.0 * grad_var * convolved) / valid_count).astype(jnp.bfloat16)
        grad_padded = jnp.pad(grad_conv, ((KERNEL // 2, KERNEL // 2), (0, 0)))
        grad_gated, grad_depth = depth_back(grad_padded, grad_conv, padded, depth)
        grad_mixed = jnp.concatenate([token_mask * grad_gated * gate_open, token_mask * grad_gated * linear * gate_open * (1.0 - gate_open)], axis=1).astype(jnp.bfloat16)
        grad_convin = jnp.dot(conv_input.T, grad_mixed, preferred_element_type=jnp.float32)
        grad_res, gain_two, shift_two = norm_backward(jnp.dot(grad_mixed, conv_in.T, preferred_element_type=jnp.float32), normed, inv_std, norm_gains[2])
        grad2 = grad3 + grad_res
        _, att_kept = attention_forward(resid1, norm_gains[1], shifts[1], attn_in, attn_out, slope, length)
        grad1, att_grads = attention_backward(grad2, att_kept, norm_gains[1], attn_in, attn_out, slope, length)
        _, ff_kept = feed_forward(resid0, norm_gains[0], shifts[0], ff_in[0], bias_in[0], ff_out[0], bias_out[0])
        grad0, ff1_grads = feed_backward(grad1, ff_kept, norm_gains[0], ff_in[0], ff_out[0])
        return (running, (grad0, ff1_grads, att_grads, grad_depth, grad_convin, gain_two, shift_two))
    _, back_out = lax.scan(back, 0.0, (clips, lengths, resids1, resids2, convs, grads3, grad_centreds))
    grads0, ff1_grads, att_grads, depth_grads, convin_grads, gain_twos, shift_twos = back_out

    def total_of(stacked):
        return lax.optimization_barrier(jnp.sum(stacked, axis=0))
    ff_in_grad = jnp.stack([total_of(ff1_grads[0]), total_of(ff2_grads[0])])
    ff_in_bias_grad = jnp.stack([total_of(ff1_grads[1]), total_of(ff2_grads[1])])
    ff_out_grad = jnp.stack([total_of(ff1_grads[2]), total_of(ff2_grads[2])])
    ff_out_bias_grad = jnp.stack([total_of(ff1_grads[3]), total_of(ff2_grads[3])])
    norm_gain_grad = jnp.stack([total_of(ff1_grads[4]), total_of(att_grads[2]), total_of(gain_twos), total_of(ff2_grads[4]), total_of(gain_fours)])
    norm_bias_grad = jnp.stack([total_of(ff1_grads[5]), total_of(att_grads[3]), total_of(shift_twos), total_of(ff2_grads[5]), total_of(shift_fours)])
    return (finals, grads0, ff_in_grad, ff_in_bias_grad, ff_out_grad, ff_out_bias_grad, total_of(att_grads[0]), total_of(att_grads[1]), total_of(convin_grads), total_of(depth_grads), total_of(convout_grads), total_of(affine_grads), norm_gain_grad, norm_bias_grad, total_of(att_grads[4]))
```

```python
import jax
import jax.numpy as jnp
from jax import lax
from jax.experimental import pallas as pl
from jax.experimental.pallas import tpu as pltpu
from jax.sharding import PartitionSpec as P

HEADS = 8
KERNEL = 31
HEAD_DIM = 64


NORM_EPS = 1e-05
SCORE_SCALE = 0.125
BF = jnp.bfloat16
F32 = jnp.float32


def mm(a, b, dims):
    return lax.dot_general(a, b, (dims, ((), ())), preferred_element_type=F32)


def mm_nn(a, b):
    return mm(a, b, ((1,), (0,)))


def mm_nt(a, b):
    return mm(a, b, ((1,), (1,)))


def mm_tn(a, b):
    return mm(a, b, ((0,), (0,)))


def shift_pairs(count, step):
    return [(j, (j + step) % count) for j in range(count)]


def gather_blocks(block, cuts, follow=None):
    count = lax.axis_size("clip")
    place = lax.axis_index("clip")
    far = range(1, count // 2)
    parts = [block] + [lax.ppermute(block, "clip", shift_pairs(count, 2 * k)) for k in far]
    if follow is not None:
        parts[1], follow = tie(parts[1], follow)
    swap = [(j, j ^ 1) for j in range(count)]
    parts += [lax.ppermute(part, "clip", swap) for part in parts]

    def kernel(spot, *refs):
        for k in range(count):
            step = 2 * (k % (count // 2))
            source = lax.rem(spot[k // (count // 2)] + (count - step), count)
            for (start, size), out in zip(cuts, refs[count:]):
                out[source] = refs[k][:, start : start + size]

    rows = block.shape[0]
    vmem = pl.BlockSpec(memory_space=pltpu.VMEM)
    blocks = pl.pallas_call(
        kernel,
        out_shape=[jax.ShapeDtypeStruct((count, rows, size), block.dtype) for _, size in cuts],
        in_specs=[pl.BlockSpec(memory_space=pltpu.SMEM)] + [vmem] * count,
        out_specs=[vmem] * len(cuts),
        name="place_blocks",
    )(jnp.stack([place, place ^ 1]).astype(jnp.int32), *parts)
    return blocks if follow is None else (blocks, follow)


def scatter_sum(blocks, axis):
    count = lax.axis_size(axis)
    place = lax.axis_index(axis)
    total = lax.dynamic_index_in_dim(blocks, place, 0, False).astype(F32)
    for k in range(1, count):
        piece = lax.dynamic_index_in_dim(blocks, (place + k) % count, 0, False)
        total = total + lax.ppermute(piece, axis, shift_pairs(count, k)).astype(F32)
    return total


def rows_to_cols(block):
    count = lax.axis_size("seq")
    place = lax.axis_index("seq")
    rows, cols = block.shape[0] // count, block.shape[1]
    mine = lax.dynamic_slice_in_dim(block, place * rows, rows, 0)
    full = jnp.zeros((rows, cols * count), block.dtype)
    full = lax.dynamic_update_slice_in_dim(full, mine, place * cols, 1)
    for k in range(1, count):
        piece = lax.dynamic_slice_in_dim(block, (place + k) % count * rows, rows, 0)
        piece = lax.ppermute(piece, "seq", shift_pairs(count, k))
        full = lax.dynamic_update_slice_in_dim(full, piece, (place - k) % count * cols, 1)
    return full


def cols_to_rows(block):
    count = lax.axis_size("seq")
    place = lax.axis_index("seq")
    rows, cols = block.shape[0], block.shape[1] // count
    mine = lax.dynamic_slice_in_dim(block, place * cols, cols, 1)
    full = jnp.zeros((rows * count, cols), block.dtype)
    full = lax.dynamic_update_slice_in_dim(full, mine, place * rows, 0)
    for k in range(1, count):
        piece = lax.dynamic_slice_in_dim(block, (place + k) % count * cols, cols, 1)
        piece = lax.ppermute(piece, "seq", shift_pairs(count, k))
        full = lax.dynamic_update_slice_in_dim(full, piece, (place - k) % count * rows, 0)
    return full


def near_sum(blocks, axis, dim=0):
    count = lax.axis_size(axis)
    low = lax.axis_index(axis) % 2
    shape = blocks.shape
    grid = blocks.reshape(shape[:dim] + (count // 2, 2) + shape[dim + 1 :])
    mine = lax.dynamic_index_in_dim(grid, low, dim + 1, False)
    other = lax.dynamic_index_in_dim(grid, 1 - low, dim + 1, False)
    other = lax.ppermute(other, axis, [(j, j ^ 1) for j in range(count)])
    return (mine.astype(F32) + other.astype(F32)).astype(BF)


def far_sum(both, axis, dim=0, behind=None):
    count = lax.axis_size(axis)
    half = count // 2
    high = lax.axis_index(axis) // 2
    total = lax.dynamic_index_in_dim(both, high, dim, False).astype(F32)
    got = []
    for k in range(1, half):
        piece = lax.dynamic_index_in_dim(both, (high + k) % half, dim, False)
        got.append(lax.ppermute(piece, axis, shift_pairs(count, 2 * k)))
    if behind is not None:
        args, got[0] = tie(behind[1], got[0])
        done = behind[0](*args)
        done, *got[1:] = tie(done, *got[1:])
    for piece in got:
        total = total + piece.astype(F32)
    return total.astype(BF) if behind is None else (total.astype(BF), done)


def owners(grad, rows, cols):
    return grad.reshape(lax.axis_size("clip"), lax.axis_size("seq"), rows, cols)


def tie(value, *others):
    return lax.optimization_barrier((value,) + others)


def total_all(rows):
    count = lax.axis_size("clip") * lax.axis_size("seq")
    spread = jnp.broadcast_to(rows[None], (count,) + rows.shape)
    return jnp.sum(lax.all_to_all(spread, ("clip", "seq"), 0, 0, tiled=True), axis=0)


def with_halo(block):
    count = lax.axis_size("seq")
    forward = [(i, i + 1) for i in range(count - 1)]
    backward = [(target, source) for source, target in forward]
    low = lax.ppermute(block[block.shape[0] - HALO :], "seq", forward)
    high = lax.ppermute(block[:HALO], "seq", backward)
    return (low, block, high)


def swish(values):
    return values * jax.nn.sigmoid(values)


def swish_slope(values):
    sigmoid_v = jax.nn.sigmoid(values)
    return sigmoid_v * (1.0 + values * (1.0 - sigmoid_v))


def norm_forward(resid, gain, shift):
    average = jnp.mean(resid, axis=-1, keepdims=True)
    centred = resid - average
    variance = jnp.mean(centred * centred, axis=-1, keepdims=True)
    inv_std = lax.rsqrt(variance + NORM_EPS)
    normed = centred * inv_std
    return (normed * gain + shift, normed, inv_std)


def norm_backward(cotangent, normed, inv_std, gain):
    scaled = cotangent * gain
    inner_sum = (
        scaled
        - jnp.mean(scaled, axis=-1, keepdims=True)
        - normed * jnp.mean(scaled * normed, axis=-1, keepdims=True)
    )
    return (inv_std * inner_sum, jnp.sum(cotangent * normed, axis=0), jnp.sum(cotangent, axis=0))


HALO = 16
LANES = 128


def load_padded(buf, low, block, high):
    rows = block.shape[0]
    buf[0:HALO, :] = low[...].astype(F32)
    buf[HALO : HALO + rows, :] = block[...].astype(F32)
    buf[HALO + rows : 2 * HALO + rows, :] = high[...].astype(F32)


def conv_kernel(low, block, high, mask, depth, conv, stats, buf):
    rows, width = block.shape
    load_padded(buf, low, block, high)
    keep = mask[...]
    for start in range(0, width, LANES):
        cols = slice(start, start + LANES)
        total = jnp.zeros((rows, LANES), F32)
        for low_bits in range(8):
            shifted = buf[low_bits : low_bits + rows + 24, cols]
            for high_bits in range(4):
                tap = 8 * high_bits + low_bits - 1
                if 0 <= tap < KERNEL:
                    total = total + depth[tap : tap + 1, cols] * shifted[
                        8 * high_bits : 8 * high_bits + rows
                    ]
        conv[:, cols] = total
        kept = keep * total
        stats[0:1, cols] = jnp.sum(kept, axis=0, keepdims=True)
        stats[1:2, cols] = jnp.sum(kept * total, axis=0, keepdims=True)
        stats[2:3, cols] = jnp.broadcast_to(jnp.sum(keep, axis=0, keepdims=True), (1, LANES))


def depth_conv(low, block, high, mask, depth):
    rows, width = block.shape
    return pl.pallas_call(
        conv_kernel,
        out_shape=(
            jax.ShapeDtypeStruct((rows, width), F32),
            jax.ShapeDtypeStruct((3, width), F32),
        ),
        scratch_shapes=[pltpu.VMEM((rows + 2 * HALO, width), F32)],
        name="depth_conv",
    )(low, block, high, mask, depth)


def back_kernel(
    low, block, high, glow, gblock, ghigh, mask, linear, gate, depth, gmixed, gdepth, buf, gbuf
):
    rows, width = block.shape
    load_padded(buf, low, block, high)
    load_padded(gbuf, glow, gblock, ghigh)
    keep = mask[...]
    for start in range(0, width, LANES):
        cols = slice(start, start + LANES)
        here = gblock[:, cols].astype(F32)
        total = jnp.zeros((rows, LANES), F32)
        for low_bits in range(8):
            shifted = buf[low_bits : low_bits + rows + 24, cols]
            gshifted = gbuf[low_bits : low_bits + rows + 24, cols]
            for high_bits in range(4):
                span = slice(8 * high_bits, 8 * high_bits + rows)
                step = 8 * high_bits + low_bits
                tap = step - 1
                if 0 <= tap < KERNEL:
                    gdepth[tap : tap + 1, cols] = jnp.sum(
                        here * shifted[span], axis=0, keepdims=True
                    )
                tap = KERNEL - step
                if 0 <= tap < KERNEL:
                    total = total + depth[tap : tap + 1, cols] * gshifted[span]
        total = keep * total
        open_v = gate[:, cols]
        first = total * open_v
        gmixed[:, cols] = first.astype(BF)
        gmixed[:, width + start : width + start + LANES] = (
            first * linear[:, cols] * (1.0 - open_v)
        ).astype(BF)


def depth_back(padded, grads, mask, linear, gate, depth):
    rows, width = linear.shape
    return pl.pallas_call(
        back_kernel,
        out_shape=(
            jax.ShapeDtypeStruct((rows, 2 * width), BF),
            jax.ShapeDtypeStruct((KERNEL, width), F32),
        ),
        scratch_shapes=[pltpu.VMEM((rows + 2 * HALO, width), F32)] * 2,
        name="depth_back",
    )(*padded, *grads, mask, linear, gate, depth)


def head_split(cols):
    return [cols[:, i : i + HEAD_DIM] for i in range(0, cols.shape[1], HEAD_DIM)]


def on_device(
    clips,
    lengths,
    ff_in,
    ff_in_bias,
    ff_out,
    ff_out_bias,
    attn_in,
    attn_out,
    conv_in,
    conv_depth,
    conv_out,
    bn_affine,
    norm_gain,
    norm_bias,
    slope,
    out_grad,
):
    clip_count = lax.axis_size("clip")
    seq_count = lax.axis_size("seq")
    place = lax.axis_index("seq")
    rows = clips.shape[1]
    tokens = rows * seq_count
    width = clips.shape[2]
    hidden = ff_in.shape[2]
    d_rows = ff_in.shape[1]
    h_rows = ff_out.shape[1]
    h_part = h_rows // seq_count
    d_part = d_rows // seq_count
    head_cols = width // seq_count
    head_count = HEADS // seq_count

    sub = clip_count * h_part
    ins = [w.reshape(d_rows, clip_count, seq_count, h_part) for w in (ff_in[0], ff_in[1])]
    ins = [lax.dynamic_index_in_dim(w, place, 2, False).reshape(d_rows, sub) for w in ins]
    outs = lax.dynamic_slice_in_dim(ff_out, place * h_part, h_part, 1)
    smalls = jnp.concatenate(
        [
            ff_out_bias,
            bn_affine,
            norm_gain,
            norm_bias,
            conv_depth,
            ff_in_bias.reshape(2 * h_rows // d_rows, d_rows),
        ],
        axis=0,
    )
    small_rows = smalls.shape[0]
    qkv = lax.dynamic_slice_in_dim(attn_in, place * head_cols, head_cols, 2)
    p_rows = max(d_rows, h_part)
    lanes = pl.cdiv(small_rows, LANES) * LANES

    def padded_to(block, cols):
        return jnp.pad(block, ((0, p_rows - block.shape[0]), (0, cols - block.shape[1])))

    first = jnp.concatenate(
        [padded_to(ins[0], sub), padded_to(outs[0], width), padded_to(smalls.T, lanes)]
        + [padded_to(qkv[i], head_cols) for i in range(3)],
        axis=1,
    )
    sizes = [sub, width, lanes, 3 * head_cols]
    cuts = [(sum(sizes[:i]), size) for i, size in enumerate(sizes)]
    late = jnp.concatenate(
        [padded_to(attn_out, width), padded_to(conv_in, conv_in.shape[1])]
        + [padded_to(conv_out, width), padded_to(ins[1], sub), padded_to(outs[1], width)],
        axis=1,
    )
    got, late = gather_blocks(first, cuts, late)
    got_in0 = got[0][:, :d_rows].reshape(width, sub)
    got_out0 = got[1][:, :h_part].reshape(sub, width)
    got_small = got[2][:, :d_rows].reshape(width, lanes)[:, :small_rows]
    w_qkv = got[3][:, :d_rows].reshape(width, 3 * head_cols)

    c_cols = conv_in.shape[1]
    sizes = [width, c_cols, width, sub, width]
    cuts = [(sum(sizes[:i]), size) for i, size in enumerate(sizes)]
    got = gather_blocks(late, cuts)
    w_attnout, w_convin, w_convout = [w[:, :d_rows].reshape(width, -1) for w in got[:3]]
    got_in1 = got[3][:, :d_rows].reshape(width, sub)
    got_out1 = got[4][:, :h_part].reshape(sub, width)

    lines = got_small.astype(F32).T
    n_vec = small_rows - 2 * h_rows // d_rows
    ffout_bias = lines[0:2]
    affine = lines[2:4]
    norm_gains = lines[4:9]
    shifts = lines[9:14]
    w_depth = lines[14:n_vec]
    bias_in = lines[n_vec:].reshape(2, h_rows // d_rows, clip_count, d_rows)
    bias_in = bias_in.transpose(0, 2, 1, 3).reshape(2, hidden)
    bias_in = bias_in.reshape(2, clip_count, seq_count, h_part)
    bias_in = lax.dynamic_index_in_dim(bias_in, place, 2, False).reshape(2, sub)

    length = lengths[0]
    positions = place * rows + jnp.arange(rows, dtype=jnp.int32)
    token_mask = (positions < length).astype(F32)[:, None]
    head_slope = lax.dynamic_slice_in_dim(slope, place * head_count, head_count, 0)

    clips_all = lax.all_gather(clips[0], "seq", axis=0, tiled=True)
    ffin0 = norm_forward(clips_all.astype(F32), norm_gains[0], shifts[0])[0].astype(BF)
    resid0 = clips[0].astype(F32)
    _, normed0, inv0 = norm_forward(resid0, norm_gains[0], shifts[0])
    pre0 = mm_nn(ffin0, got_in0) + bias_in[0]
    hid0 = swish(pre0).astype(BF)
    part = mm_nn(hid0, got_out0).astype(BF)
    resid1 = resid0 + 0.5 * (
        scatter_sum(part.reshape(seq_count, rows, width), "seq") + ffout_bias[0]
    )

    att_norm, normed1, inv1 = norm_forward(resid1, norm_gains[1], shifts[1])
    attin = lax.all_gather(att_norm.astype(BF), "seq", axis=0, tiled=True)
    qkv_all = mm_nn(attin, w_qkv).astype(BF)
    q_heads = head_split(qkv_all[:, :head_cols])
    k_heads = head_split(qkv_all[:, head_cols : 2 * head_cols])
    v_heads = head_split(qkv_all[:, 2 * head_cols :])
    spot = jnp.arange(tokens, dtype=jnp.int32)
    distance = jnp.log1p(jnp.abs(spot[:, None] - spot[None, :]).astype(F32))
    key_ok = (spot < length)[None, :]
    probs = []
    head_outs = []
    for h in range(head_count):
        scores = mm_nt(q_heads[h], k_heads[h]) * SCORE_SCALE - head_slope[h] * distance
        scores = jnp.where(key_ok, scores, -jnp.inf)
        highest = jnp.max(scores, axis=-1, keepdims=True)
        log_total = highest + jnp.log(jnp.sum(jnp.exp(scores - highest), axis=-1, keepdims=True))
        prob = jnp.exp(scores - log_total)
        probs.append(prob)
        head_outs.append(mm_nn(prob.astype(BF), v_heads[h]).astype(BF))
    head_out = jnp.concatenate(head_outs, axis=1)
    att_tok = rows_to_cols(head_out)
    resid2 = resid1 + mm_nn(att_tok, w_attnout)

    conv_norm, normed2, inv2 = norm_forward(resid2, norm_gains[2], shifts[2])
    convin = conv_norm.astype(BF)
    mixed = mm_nn(convin, w_convin)
    linear = mixed[:, :width]
    gate = jax.nn.sigmoid(mixed[:, width:])
    gated = (token_mask * linear * gate).astype(BF)
    padded = with_halo(gated)
    conv, stats = depth_conv(*padded, token_mask, w_depth)
    stats = total_all(stats)
    count = stats[2]
    average = stats[0] / count
    variance = stats[1] / count - average * average
    batch_inv = lax.rsqrt(variance + NORM_EPS)
    centred = conv - average
    bnormed = centred * batch_inv
    batch_out = bnormed * affine[0] + affine[1]
    activ = swish(batch_out).astype(BF)
    resid3 = resid2 + mm_nn(activ, w_convout)

    ff_norm, normed3, inv3 = norm_forward(resid3, norm_gains[3], shifts[3])
    ffin1 = lax.all_gather(ff_norm.astype(BF), "seq", axis=0, tiled=True)
    pre1 = mm_nn(ffin1, got_in1) + bias_in[1]
    hid1 = swish(pre1).astype(BF)
    part = mm_nn(hid1, got_out1).astype(BF)
    resid4 = resid3 + 0.5 * (
        scatter_sum(part.reshape(seq_count, rows, width), "seq") + ffout_bias[1]
    )
    final, normed4, inv4 = norm_forward(resid4, norm_gains[4], shifts[4])

    grad4, gain4, shift4 = norm_backward(out_grad[0].astype(F32), normed4, inv4, norm_gains[4])
    half1 = 0.5 * grad4
    g_bout1 = jnp.sum(half1, axis=0)
    half1_all = lax.all_gather(half1.astype(BF), "seq", axis=0, tiled=True)
    gpre1 = mm_nt(half1_all, got_out1) * swish_slope(pre1)
    gpre1_b = gpre1.astype(BF)
    g_bin1 = jnp.sum(gpre1, axis=0)
    part = mm_nt(gpre1_b, got_in1).astype(BF)
    g_ffin = scatter_sum(part.reshape(seq_count, rows, width), "seq")
    back, gain3, shift3 = norm_backward(g_ffin, normed3, inv3, norm_gains[3])
    grad3 = grad4 + back
    grad3_b = grad3.astype(BF)
    g_out1 = mm_tn(hid1, half1_all).astype(BF)
    g_in1 = mm_tn(ffin1, gpre1_b).astype(BF)
    g_convout = mm_tn(activ, grad3_b).astype(BF)
    groups = clip_count * seq_count
    wide = max(sub, width)

    def fit(block):
        spare = wide - block.shape[-1]
        return jnp.pad(block, [(0, 0)] * (block.ndim - 1) + [(0, spare)]) if spare else block

    def ff_pack(g_in, g_out):
        return [
            fit(g_in.reshape(clip_count, d_rows, sub)),
            fit(g_out.reshape(clip_count, h_part, width)),
        ]

    near1 = near_sum(jnp.concatenate(ff_pack(g_in1, g_out1), axis=1), "clip")

    gbn = mm_nt(grad3_b, w_convout) * swish_slope(batch_out)
    g_affine = jnp.stack([jnp.sum(gbn * bnormed, axis=0), jnp.sum(gbn, axis=0)])
    gcent = gbn * affine[0]
    sums = total_all(jnp.stack([jnp.sum(gcent, axis=0), jnp.sum(gcent * centred, axis=0)]))
    sums, near1 = tie(sums, near1)
    own1 = far_sum(near1, "clip")
    grad_var = -0.5 * batch_inv**3 * sums[1]
    grad_avg = -batch_inv * sums[0] - 2.0 * average * grad_var
    gconv = (
        gcent * batch_inv + token_mask * (grad_avg + 2.0 * grad_var * conv) / count
    ).astype(BF)
    gmixed, g_depth = depth_back(padded, with_halo(gconv), token_mask, linear, gate, w_depth)
    back, gain2, shift2 = norm_backward(mm_nt(gmixed, w_convin), normed2, inv2, norm_gains[2])
    grad2 = grad3 + back
    grad2_b = grad2.astype(BF)
    gatt = mm_nt(grad2_b, w_attnout).astype(BF)
    gatt_all = cols_to_rows(gatt)
    g_convin = mm_tn(convin, gmixed).astype(BF)
    g_attnout = mm_tn(att_tok, grad2_b).astype(BF)
    g_mixed = jnp.concatenate([g_convout, g_attnout, g_convin], axis=1)
    m_cols = g_mixed.shape[1]
    core_c = near_sum(owners(g_mixed, d_part, m_cols), "seq", 1)

    grad_q = []
    grad_k = []
    grad_v = []
    grad_slope = []
    for h, g_head in enumerate(head_split(gatt_all)):
        prob = probs[h]
        gprob = mm_nt(g_head, v_heads[h])
        inner = jnp.sum(prob * gprob, axis=-1, keepdims=True)
        gscore = prob * (gprob - inner)
        grad_slope.append(-jnp.sum(gscore * distance))
        gscore_b = gscore.astype(BF)
        grad_q.append((SCORE_SCALE * mm_nn(gscore_b, k_heads[h])).astype(BF))
        grad_k.append((SCORE_SCALE * mm_tn(gscore_b, q_heads[h])).astype(BF))
        grad_v.append(mm_tn(prob.astype(BF), g_head).astype(BF))
    gqkv = jnp.concatenate(grad_q + grad_k + grad_v, axis=1)
    gqkv, own1, core_c = tie(gqkv, own1, core_c)
    row_c = far_sum(core_c, "seq", 1)
    part = mm_nt(gqkv, w_qkv).astype(BF)
    g_attin = scatter_sum(part.reshape(seq_count, rows, width), "seq")
    g_qkv = mm_tn(attin, gqkv).astype(BF)
    near_q = near_sum(g_qkv.reshape(clip_count, d_rows, 3 * head_cols), "clip")
    g_attin, row_c = tie(g_attin, row_c)
    near_c = near_sum(row_c, "clip")
    back, gain1, shift1 = norm_backward(g_attin, normed1, inv1, norm_gains[1])
    grad1 = grad2 + back

    half0 = 0.5 * grad1
    g_bout0 = jnp.sum(half0, axis=0)
    half0_all = lax.all_gather(half0.astype(BF), "seq", axis=0, tiled=True)
    gpre0 = mm_nt(half0_all, got_out0) * swish_slope(pre0)
    gpre0_b = gpre0.astype(BF)
    g_bin0 = jnp.sum(gpre0, axis=0)
    gpre0_b, near_q, near_c = tie(gpre0_b, near_q, near_c)
    own_qkv = far_sum(near_q, "clip")
    own_c = far_sum(near_c, "clip")
    g_out0 = mm_tn(hid0, half0_all).astype(BF)
    g_in0 = mm_tn(ffin0, gpre0_b).astype(BF)

    bin_full = jnp.zeros((clip_count, 2, seq_count, h_part), F32)
    bin_full = lax.dynamic_update_slice_in_dim(
        bin_full,
        jnp.stack([g_bin0, g_bin1]).reshape(2, clip_count, 1, h_part).transpose(1, 0, 2, 3),
        place,
        2,
    )
    sum_lines = jnp.concatenate(
        [
            jnp.stack([g_bout0, g_bout1]),
            g_affine,
            jnp.stack([gain1, gain2, gain3, gain4, shift1, shift2, shift3, shift4]),
            g_depth,
        ],
        axis=0,
    )
    n_lines = sum_lines.shape[0]
    sum_pack = jnp.concatenate(
        [
            sum_lines.reshape(n_lines, clip_count, d_rows).transpose(1, 0, 2),
            bin_full.reshape(clip_count, 2 * h_rows // d_rows, d_rows),
        ],
        axis=1,
    ).astype(BF)
    n_small = sum_pack.shape[1] * d_rows
    s_rows = pl.cdiv(n_small, width)
    sum_pack = jnp.pad(
        sum_pack.reshape(clip_count, n_small), ((0, 0), (0, s_rows * width - n_small))
    ).reshape(clip_count, s_rows, width)
    near0 = near_sum(
        jnp.concatenate(
            ff_pack(g_in0, g_out0) + [fit(sum_pack)],
            axis=1,
        ),
        "clip",
    )
    part = mm_nt(gpre0_b, got_in0).astype(BF)
    g_ffin = scatter_sum(part.reshape(seq_count, rows, width), "seq")
    g_ffin, near0 = tie(g_ffin, near0)

    def early(share1, share_qkv, share_c):
        share1 = jnp.concatenate([share1, fit(share_qkv)], axis=0)
        return tuple(lax.all_gather(x, "seq", axis=0) for x in (share1, share_c))

    own0, (all1, all_c) = far_sum(near0, "clip", behind=(early, (own1, own_qkv, own_c)))

    back, gain0, shift0 = norm_backward(g_ffin, normed0, inv0, norm_gains[0])
    grad0 = grad1 + back
    slope_full = lax.dynamic_update_slice_in_dim(
        jnp.zeros((HEADS,), F32), jnp.stack(grad_slope), place * head_count, 0
    )
    last = jnp.concatenate(
        [gain0.reshape(clip_count, d_rows), shift0.reshape(clip_count, d_rows)], axis=1
    )
    slope_rows = jnp.zeros((clip_count, 2 * d_rows), F32).at[:, :HEADS].set(slope_full)
    last = jnp.stack([last, slope_rows], axis=1)
    last = jnp.broadcast_to(last[:, None], (clip_count, seq_count) + last.shape[1:])
    last = lax.all_to_all(
        last.reshape((groups,) + last.shape[2:]), ("clip", "seq"), 0, 0, tiled=True
    )
    last = jnp.sum(last, axis=0)
    slope_total = last[1, :HEADS]
    gain0_own = last[0, :d_rows]
    shift0_own = last[0, d_rows:]

    all_c = all_c.reshape(d_rows, m_cols).astype(F32)
    all0 = lax.all_gather(own0, "seq", axis=0)
    all_small = all0[:, d_rows + h_part : d_rows + h_part + s_rows, :width]
    all_small = jnp.sum(all_small.astype(F32), axis=0)
    all_small = all_small.reshape(-1)[:n_small].reshape(n_small // d_rows, d_rows)
    all_qkv = all1[:, d_rows + h_part :, : 3 * head_cols]

    def ff_grads(full):
        g_in = full[:, :d_rows, :sub].reshape(seq_count, d_rows, clip_count, h_part)
        g_in = g_in.transpose(1, 2, 0, 3).reshape(d_rows, hidden)
        g_out = full[:, d_rows : d_rows + h_part, :width].reshape(h_rows, width)
        return (g_in.astype(F32), g_out.astype(F32))

    o_in0, o_out0 = ff_grads(all0)
    o_in1, o_out1 = ff_grads(all1)
    o_convout = all_c[:, :width]
    o_attnout = all_c[:, width : 2 * width]
    o_convin = all_c[:, 2 * width :]
    o_attn = (
        all_qkv.reshape(seq_count, d_rows, 3, head_cols)
        .transpose(2, 1, 0, 3)
        .reshape(3, d_rows, width)
        .astype(F32)
    )
    o_bin = all_small[n_lines:].reshape(2, h_rows)
    o_gain = jnp.concatenate([gain0_own[None], all_small[4:8]], axis=0)
    o_shift = jnp.concatenate([shift0_own[None], all_small[8:12]], axis=0)
    return (
        final.astype(BF)[None],
        grad0[None],
        jnp.stack([o_in0, o_in1]),
        o_bin,
        jnp.stack([o_out0, o_out1]),
        all_small[0:2],
        o_attn,
        o_attnout,
        o_convin,
        all_small[12:n_lines],
        o_convout,
        all_small[2:4],
        o_gain,
        o_shift,
        slope_total,
    )


def solution(mesh):
    in_specs = (
        P("clip", "seq", None),
        P("clip"),
        P(None, "clip", None),
        P(None, "clip"),
        P(None, "clip", None),
        P(None, "clip"),
        P(None, "clip", None),
        P("clip", None),
        P("clip", None),
        P(None, "clip"),
        P("clip", None),
        P(None, "clip"),
        P(None, "clip"),
        P(None, "clip"),
        P(),
        P("clip", "seq", None),
    )
    out_specs = (
        P("clip", "seq", None),
        P("clip", "seq", None),
        P(None, "clip", None),
        P(None, "clip"),
        P(None, "clip", None),
        P(None, "clip"),
        P(None, "clip", None),
        P("clip", None),
        P("clip", None),
        P(None, "clip"),
        P("clip", None),
        P(None, "clip"),
        P(None, "clip"),
        P(None, "clip"),
        P(),
    )
    return jax.shard_map(
        on_device, mesh=mesh, in_specs=in_specs, out_specs=out_specs, check_vma=False
    )
```

```python
import jax
import jax.numpy as jnp
from jax import lax
from jax.experimental import pallas as pl
from jax.experimental.pallas import tpu as pltpu
from jax.sharding import PartitionSpec as P

HEADS = 8
KERNEL = 31
HEAD_DIM = 64


NORM_EPS = 1e-05
SCORE_SCALE = 0.125
BF = jnp.bfloat16
F32 = jnp.float32


def mm(a, b, dims):
    return lax.dot_general(a, b, (dims, ((), ())), preferred_element_type=F32)


def mm_nn(a, b):
    return mm(a, b, ((1,), (0,)))


def mm_nt(a, b):
    return mm(a, b, ((1,), (1,)))


def mm_tn(a, b):
    return mm(a, b, ((0,), (0,)))


def shift_pairs(count, step):
    return [(j, (j + step) % count) for j in range(count)]


def far_parts(block):
    count = lax.axis_size("clip")
    far = range(1, count // 2)
    return [block] + [lax.ppermute(block, "clip", shift_pairs(count, 2 * k)) for k in far]


def place_parts(parts, cuts):
    count = lax.axis_size("clip")
    place = lax.axis_index("clip")
    swap = [(j, j ^ 1) for j in range(count)]
    parts = parts + [lax.ppermute(part, "clip", swap) for part in parts]
    rows, dtype = parts[0].shape[0], parts[0].dtype

    def kernel(spot, *refs):
        for k in range(count):
            step = 2 * (k % (count // 2))
            source = lax.rem(spot[k // (count // 2)] + (count - step), count)
            for (start, size), out in zip(cuts, refs[count:]):
                out[source] = refs[k][:, start : start + size]

    vmem = pl.BlockSpec(memory_space=pltpu.VMEM)
    return pl.pallas_call(
        kernel,
        out_shape=[jax.ShapeDtypeStruct((count, rows, size), dtype) for _, size in cuts],
        in_specs=[pl.BlockSpec(memory_space=pltpu.SMEM)] + [vmem] * count,
        out_specs=[vmem] * len(cuts),
        name="place_blocks",
    )(jnp.stack([place, place ^ 1]).astype(jnp.int32), *parts)


def scatter_sum(blocks, axis):
    count = lax.axis_size(axis)
    place = lax.axis_index(axis)
    total = lax.dynamic_index_in_dim(blocks, place, 0, False).astype(F32)
    for k in range(1, count):
        piece = lax.dynamic_index_in_dim(blocks, (place + k) % count, 0, False)
        total = total + lax.ppermute(piece, axis, shift_pairs(count, k)).astype(F32)
    return total


def rows_to_cols(block):
    count = lax.axis_size("seq")
    place = lax.axis_index("seq")
    rows, cols = block.shape[0] // count, block.shape[1]
    mine = lax.dynamic_slice_in_dim(block, place * rows, rows, 0)
    full = jnp.zeros((rows, cols * count), block.dtype)
    full = lax.dynamic_update_slice_in_dim(full, mine, place * cols, 1)
    for k in range(1, count):
        piece = lax.dynamic_slice_in_dim(block, (place + k) % count * rows, rows, 0)
        piece = lax.ppermute(piece, "seq", shift_pairs(count, k))
        full = lax.dynamic_update_slice_in_dim(full, piece, (place - k) % count * cols, 1)
    return full


def cols_to_rows(block):
    count = lax.axis_size("seq")
    place = lax.axis_index("seq")
    rows, cols = block.shape[0], block.shape[1] // count
    mine = lax.dynamic_slice_in_dim(block, place * cols, cols, 1)
    full = jnp.zeros((rows * count, cols), block.dtype)
    full = lax.dynamic_update_slice_in_dim(full, mine, place * rows, 0)
    for k in range(1, count):
        piece = lax.dynamic_slice_in_dim(block, (place + k) % count * cols, cols, 1)
        piece = lax.ppermute(piece, "seq", shift_pairs(count, k))
        full = lax.dynamic_update_slice_in_dim(full, piece, (place - k) % count * rows, 0)
    return full


def near_sum(blocks, axis, dim=0):
    count = lax.axis_size(axis)
    low = lax.axis_index(axis) % 2
    shape = blocks.shape
    grid = blocks.reshape(shape[:dim] + (count // 2, 2) + shape[dim + 1 :])
    mine = lax.dynamic_index_in_dim(grid, low, dim + 1, False)
    other = lax.dynamic_index_in_dim(grid, 1 - low, dim + 1, False)
    other = lax.ppermute(other, axis, [(j, j ^ 1) for j in range(count)])
    return (mine.astype(F32) + other.astype(F32)).astype(BF)


def far_sum(both, axis, dim=0):
    count = lax.axis_size(axis)
    half = count // 2
    high = lax.axis_index(axis) // 2
    total = lax.dynamic_index_in_dim(both, high, dim, False).astype(F32)
    got = []
    for k in range(1, half):
        piece = lax.dynamic_index_in_dim(both, (high + k) % half, dim, False)
        got.append(lax.ppermute(piece, axis, shift_pairs(count, 2 * k)))
    for piece in got:
        total = total + piece.astype(F32)
    return total.astype(BF)


def owners(grad, rows, cols):
    return grad.reshape(lax.axis_size("clip"), lax.axis_size("seq"), rows, cols)


def tie(value, *others):
    return lax.optimization_barrier((value,) + others)


def total_all(rows):
    count = lax.axis_size("clip") * lax.axis_size("seq")
    spread = jnp.broadcast_to(rows[None], (count,) + rows.shape)
    return jnp.sum(lax.all_to_all(spread, ("clip", "seq"), 0, 0, tiled=True), axis=0)


def with_halo(block):
    count = lax.axis_size("seq")
    forward = [(i, i + 1) for i in range(count - 1)]
    backward = [(target, source) for source, target in forward]
    low = lax.ppermute(block[block.shape[0] - HALO :], "seq", forward)
    high = lax.ppermute(block[:HALO], "seq", backward)
    return (low, block, high)


def swish(values):
    return values * jax.nn.sigmoid(values)


def swish_slope(values):
    sigmoid_v = jax.nn.sigmoid(values)
    return sigmoid_v * (1.0 + values * (1.0 - sigmoid_v))


def norm_forward(resid, gain, shift):
    average = jnp.mean(resid, axis=-1, keepdims=True)
    centred = resid - average
    variance = jnp.mean(centred * centred, axis=-1, keepdims=True)
    inv_std = lax.rsqrt(variance + NORM_EPS)
    normed = centred * inv_std
    return (normed * gain + shift, normed, inv_std)


def norm_backward(cotangent, normed, inv_std, gain):
    scaled = cotangent * gain
    inner_sum = (
        scaled
        - jnp.mean(scaled, axis=-1, keepdims=True)
        - normed * jnp.mean(scaled * normed, axis=-1, keepdims=True)
    )
    return (inv_std * inner_sum, jnp.sum(cotangent * normed, axis=0), jnp.sum(cotangent, axis=0))


HALO = 16
LANES = 128


def load_padded(buf, low, block, high):
    rows = block.shape[0]
    buf[0:HALO, :] = low[...].astype(F32)
    buf[HALO : HALO + rows, :] = block[...].astype(F32)
    buf[HALO + rows : 2 * HALO + rows, :] = high[...].astype(F32)


def conv_kernel(low, block, high, mask, depth, conv, stats, buf):
    rows, width = block.shape
    load_padded(buf, low, block, high)
    keep = mask[...]

    @pl.loop(0, width // LANES)
    def _(step):
        cols = pl.ds(pl.multiple_of(step * LANES, LANES), LANES)
        total = jnp.zeros((rows, LANES), F32)
        for low_bits in range(8):
            shifted = buf[low_bits : low_bits + rows + 24, cols]
            for high_bits in range(4):
                tap = 8 * high_bits + low_bits - 1
                if 0 <= tap < KERNEL:
                    total = total + depth[tap : tap + 1, cols] * shifted[
                        8 * high_bits : 8 * high_bits + rows
                    ]
        conv[:, cols] = total
        kept = keep * total
        stats[0:1, cols] = jnp.sum(kept, axis=0, keepdims=True)
        stats[1:2, cols] = jnp.sum(kept * total, axis=0, keepdims=True)
        stats[2:3, cols] = jnp.broadcast_to(jnp.sum(keep, axis=0, keepdims=True), (1, LANES))


def depth_conv(low, block, high, mask, depth):
    rows, width = block.shape
    return pl.pallas_call(
        conv_kernel,
        out_shape=(
            jax.ShapeDtypeStruct((rows, width), F32),
            jax.ShapeDtypeStruct((3, width), F32),
        ),
        scratch_shapes=[pltpu.VMEM((rows + 2 * HALO, width), F32)],
        name="depth_conv",
    )(low, block, high, mask, depth)


def back_kernel(
    low, block, high, glow, gblock, ghigh, mask, linear, gate, depth, gmixed, gdepth, buf, gbuf
):
    rows, width = block.shape
    load_padded(buf, low, block, high)
    load_padded(gbuf, glow, gblock, ghigh)
    keep = mask[...]

    @pl.loop(0, width // LANES)
    def _(block_step):
        start = pl.multiple_of(block_step * LANES, LANES)
        cols = pl.ds(start, LANES)
        here = gblock[:, cols].astype(F32)
        total = jnp.zeros((rows, LANES), F32)
        for low_bits in range(8):
            shifted = buf[low_bits : low_bits + rows + 24, cols]
            gshifted = gbuf[low_bits : low_bits + rows + 24, cols]
            for high_bits in range(4):
                span = slice(8 * high_bits, 8 * high_bits + rows)
                step = 8 * high_bits + low_bits
                tap = step - 1
                if 0 <= tap < KERNEL:
                    gdepth[tap : tap + 1, cols] = jnp.sum(
                        here * shifted[span], axis=0, keepdims=True
                    )
                tap = KERNEL - step
                if 0 <= tap < KERNEL:
                    total = total + depth[tap : tap + 1, cols] * gshifted[span]
        total = keep * total
        open_v = gate[:, cols]
        first = total * open_v
        gmixed[:, cols] = first.astype(BF)
        gmixed[:, pl.ds(pl.multiple_of(width + start, LANES), LANES)] = (
            first * linear[:, cols] * (1.0 - open_v)
        ).astype(BF)


def depth_back(padded, grads, mask, linear, gate, depth):
    rows, width = linear.shape
    return pl.pallas_call(
        back_kernel,
        out_shape=(
            jax.ShapeDtypeStruct((rows, 2 * width), BF),
            jax.ShapeDtypeStruct((KERNEL, width), F32),
        ),
        scratch_shapes=[pltpu.VMEM((rows + 2 * HALO, width), F32)] * 2,
        name="depth_back",
    )(*padded, *grads, mask, linear, gate, depth)


def head_split(cols):
    return [cols[:, i : i + HEAD_DIM] for i in range(0, cols.shape[1], HEAD_DIM)]


def on_device(
    clips,
    lengths,
    ff_in,
    ff_in_bias,
    ff_out,
    ff_out_bias,
    attn_in,
    attn_out,
    conv_in,
    conv_depth,
    conv_out,
    bn_affine,
    norm_gain,
    norm_bias,
    slope,
    out_grad,
):
    clip_count = lax.axis_size("clip")
    seq_count = lax.axis_size("seq")
    place = lax.axis_index("seq")
    rows = clips.shape[1]
    tokens = rows * seq_count
    width = clips.shape[2]
    hidden = ff_in.shape[2]
    d_rows = ff_in.shape[1]
    h_rows = ff_out.shape[1]
    h_part = h_rows // seq_count
    d_part = d_rows // seq_count
    head_cols = width // seq_count
    head_count = HEADS // seq_count

    sub = clip_count * h_part
    ins = [w.reshape(d_rows, clip_count, seq_count, h_part) for w in (ff_in[0], ff_in[1])]
    ins = [lax.dynamic_index_in_dim(w, place, 2, False).reshape(d_rows, sub) for w in ins]
    outs = lax.dynamic_slice_in_dim(ff_out, place * h_part, h_part, 1)
    smalls = jnp.concatenate(
        [
            ff_out_bias,
            bn_affine,
            norm_gain,
            norm_bias,
            conv_depth,
            ff_in_bias.reshape(2 * h_rows // d_rows, d_rows),
        ],
        axis=0,
    )
    small_rows = smalls.shape[0]
    qkv = lax.dynamic_slice_in_dim(attn_in, place * head_cols, head_cols, 2)
    p_rows = max(d_rows, h_part)
    lanes = pl.cdiv(small_rows, LANES) * LANES

    def padded_to(block, cols):
        return jnp.pad(block, ((0, p_rows - block.shape[0]), (0, cols - block.shape[1])))

    first = jnp.concatenate(
        [padded_to(ins[0], sub), padded_to(outs[0], width), padded_to(smalls.T, lanes)]
        + [padded_to(qkv[i], head_cols) for i in range(3)],
        axis=1,
    )
    sizes = [sub, width, lanes, 3 * head_cols]
    cuts = [(sum(sizes[:i]), size) for i, size in enumerate(sizes)]
    late = jnp.concatenate(
        [padded_to(attn_out, width), padded_to(conv_in, conv_in.shape[1])]
        + [padded_to(conv_out, width), padded_to(ins[1], sub), padded_to(outs[1], width)],
        axis=1,
    )
    first = far_parts(first)
    first[1], late = tie(first[1], late)
    late = far_parts(late)
    got = place_parts(first, cuts)
    got_in0 = got[0][:, :d_rows].reshape(width, sub)
    got_out0 = got[1][:, :h_part].reshape(sub, width)
    got_small = got[2][:, :d_rows].reshape(width, lanes)[:, :small_rows]
    w_qkv = got[3][:, :d_rows].reshape(width, 3 * head_cols)

    lines = got_small.astype(F32).T
    n_vec = small_rows - 2 * h_rows // d_rows
    ffout_bias = lines[0:2]
    affine = lines[2:4]
    norm_gains = lines[4:9]
    shifts = lines[9:14]
    w_depth = lines[14:n_vec]
    bias_in = lines[n_vec:].reshape(2, h_rows // d_rows, clip_count, d_rows)
    bias_in = bias_in.transpose(0, 2, 1, 3).reshape(2, hidden)
    bias_in = bias_in.reshape(2, clip_count, seq_count, h_part)
    bias_in = lax.dynamic_index_in_dim(bias_in, place, 2, False).reshape(2, sub)

    length = lengths[0]
    positions = place * rows + jnp.arange(rows, dtype=jnp.int32)
    token_mask = (positions < length).astype(F32)[:, None]
    head_slope = lax.dynamic_slice_in_dim(slope, place * head_count, head_count, 0)

    clips_all = lax.all_gather(clips[0], "seq", axis=0, tiled=True)
    ffin0 = norm_forward(clips_all.astype(F32), norm_gains[0], shifts[0])[0].astype(BF)
    resid0 = clips[0].astype(F32)
    _, normed0, inv0 = norm_forward(resid0, norm_gains[0], shifts[0])
    pre0 = mm_nn(ffin0, got_in0) + bias_in[0]
    hid0 = swish(pre0).astype(BF)
    part = mm_nn(hid0, got_out0).astype(BF)
    ff_sum = scatter_sum(part.reshape(seq_count, rows, width), "seq")
    ff_sum, *late = tie(ff_sum, *late)
    resid1 = resid0 + 0.5 * (ff_sum + ffout_bias[0])
    c_cols = conv_in.shape[1]
    sizes = [width, c_cols, width, sub, width]
    cuts = [(sum(sizes[:i]), size) for i, size in enumerate(sizes)]
    got = place_parts(late, cuts)
    w_attnout, w_convin, w_convout = [w[:, :d_rows].reshape(width, -1) for w in got[:3]]
    got_in1 = got[3][:, :d_rows].reshape(width, sub)
    got_out1 = got[4][:, :h_part].reshape(sub, width)

    att_norm, normed1, inv1 = norm_forward(resid1, norm_gains[1], shifts[1])
    attin = lax.all_gather(att_norm.astype(BF), "seq", axis=0, tiled=True)
    qkv_all = mm_nn(attin, w_qkv).astype(BF)
    q_heads = head_split(qkv_all[:, :head_cols])
    k_heads = head_split(qkv_all[:, head_cols : 2 * head_cols])
    v_heads = head_split(qkv_all[:, 2 * head_cols :])
    spot = jnp.arange(tokens, dtype=jnp.int32)
    distance = jnp.log1p(jnp.abs(spot[:, None] - spot[None, :]).astype(F32))
    key_ok = (spot < length)[None, :]
    probs = []
    head_outs = []
    for h in range(head_count):
        scores = mm_nt(q_heads[h], k_heads[h]) * SCORE_SCALE - head_slope[h] * distance
        scores = jnp.where(key_ok, scores, -jnp.inf)
        highest = jnp.max(scores, axis=-1, keepdims=True)
        log_total = highest + jnp.log(jnp.sum(jnp.exp(scores - highest), axis=-1, keepdims=True))
        prob = jnp.exp(scores - log_total)
        probs.append(prob)
        head_outs.append(mm_nn(prob.astype(BF), v_heads[h]).astype(BF))
    head_out = jnp.concatenate(head_outs, axis=1)
    att_tok = rows_to_cols(head_out)
    resid2 = resid1 + mm_nn(att_tok, w_attnout)

    conv_norm, normed2, inv2 = norm_forward(resid2, norm_gains[2], shifts[2])
    convin = conv_norm.astype(BF)
    mixed = mm_nn(convin, w_convin)
    linear = mixed[:, :width]
    gate = jax.nn.sigmoid(mixed[:, width:])
    gated = (token_mask * linear * gate).astype(BF)
    padded = with_halo(gated)
    conv, stats = depth_conv(*padded, token_mask, w_depth)
    stats = total_all(stats)
    count = stats[2]
    average = stats[0] / count
    variance = stats[1] / count - average * average
    batch_inv = lax.rsqrt(variance + NORM_EPS)
    centred = conv - average
    bnormed = centred * batch_inv
    batch_out = bnormed * affine[0] + affine[1]
    activ = swish(batch_out).astype(BF)
    resid3 = resid2 + mm_nn(activ, w_convout)

    ff_norm, normed3, inv3 = norm_forward(resid3, norm_gains[3], shifts[3])
    ffin1 = lax.all_gather(ff_norm.astype(BF), "seq", axis=0, tiled=True)
    pre1 = mm_nn(ffin1, got_in1) + bias_in[1]
    hid1 = swish(pre1).astype(BF)
    part = mm_nn(hid1, got_out1).astype(BF)
    resid4 = resid3 + 0.5 * (
        scatter_sum(part.reshape(seq_count, rows, width), "seq") + ffout_bias[1]
    )
    final, normed4, inv4 = norm_forward(resid4, norm_gains[4], shifts[4])

    grad4, gain4, shift4 = norm_backward(out_grad[0].astype(F32), normed4, inv4, norm_gains[4])
    half1 = 0.5 * grad4
    g_bout1 = jnp.sum(half1, axis=0)
    half1_all = lax.all_gather(half1.astype(BF), "seq", axis=0, tiled=True)
    gpre1 = mm_nt(half1_all, got_out1) * swish_slope(pre1)
    gpre1_b = gpre1.astype(BF)
    g_bin1 = jnp.sum(gpre1, axis=0)
    part = mm_nt(gpre1_b, got_in1).astype(BF)
    g_ffin = scatter_sum(part.reshape(seq_count, rows, width), "seq")
    back, gain3, shift3 = norm_backward(g_ffin, normed3, inv3, norm_gains[3])
    grad3 = grad4 + back
    grad3_b = grad3.astype(BF)
    g_out1 = mm_tn(hid1, half1_all).astype(BF)
    g_in1 = mm_tn(ffin1, gpre1_b).astype(BF)
    g_convout = mm_tn(activ, grad3_b).astype(BF)
    groups = clip_count * seq_count
    wide = max(sub, width)

    def stack_cols(block):
        return [block[:, i : i + width] for i in range(0, block.shape[1], width)]

    def fit(block):
        spare = wide - block.shape[-1]
        return jnp.pad(block, [(0, 0)] * (block.ndim - 1) + [(0, spare)]) if spare else block

    def ff_pack(g_in, g_out):
        return [
            fit(g_in.reshape(clip_count, d_rows, sub)),
            fit(g_out.reshape(clip_count, h_part, width)),
        ]

    near1 = near_sum(jnp.concatenate(ff_pack(g_in1, g_out1), axis=1), "clip")

    gbn = mm_nt(grad3_b, w_convout) * swish_slope(batch_out)
    g_affine = jnp.stack([jnp.sum(gbn * bnormed, axis=0), jnp.sum(gbn, axis=0)])
    gcent = gbn * affine[0]
    sums = total_all(jnp.stack([jnp.sum(gcent, axis=0), jnp.sum(gcent * centred, axis=0)]))
    sums, near1 = tie(sums, near1)
    own1 = far_sum(near1, "clip")
    grad_var = -0.5 * batch_inv**3 * sums[1]
    grad_avg = -batch_inv * sums[0] - 2.0 * average * grad_var
    gconv = (
        gcent * batch_inv + token_mask * (grad_avg + 2.0 * grad_var * conv) / count
    ).astype(BF)
    gmixed, g_depth = depth_back(padded, with_halo(gconv), token_mask, linear, gate, w_depth)
    back, gain2, shift2 = norm_backward(mm_nt(gmixed, w_convin), normed2, inv2, norm_gains[2])
    grad2 = grad3 + back
    grad2_b = grad2.astype(BF)
    gatt = mm_nt(grad2_b, w_attnout).astype(BF)
    gatt_all = cols_to_rows(gatt)
    g_convin = mm_tn(convin, gmixed).astype(BF)
    g_attnout = mm_tn(att_tok, grad2_b).astype(BF)
    g_mixed = jnp.concatenate([g_convout, g_attnout, g_convin], axis=1)
    m_cols = g_mixed.shape[1]
    core_c = near_sum(owners(g_mixed, d_part, m_cols), "seq", 1)

    grad_q = []
    grad_k = []
    grad_v = []
    grad_slope = []
    for h, g_head in enumerate(head_split(gatt_all)):
        prob = probs[h]
        gprob = mm_nt(g_head, v_heads[h])
        inner = jnp.sum(prob * gprob, axis=-1, keepdims=True)
        gscore = prob * (gprob - inner)
        grad_slope.append(-jnp.sum(gscore * distance))
        gscore_b = gscore.astype(BF)
        grad_q.append((SCORE_SCALE * mm_nn(gscore_b, k_heads[h])).astype(BF))
        grad_k.append((SCORE_SCALE * mm_tn(gscore_b, q_heads[h])).astype(BF))
        grad_v.append(mm_tn(prob.astype(BF), g_head).astype(BF))
    gqkv = jnp.concatenate(grad_q + grad_k + grad_v, axis=1)
    gqkv, own1, core_c = tie(gqkv, own1, core_c)
    row_c = far_sum(core_c, "seq", 1)
    part = mm_nt(gqkv, w_qkv).astype(BF)
    g_attin = scatter_sum(part.reshape(seq_count, rows, width), "seq")
    g_qkv = mm_tn(attin, gqkv).astype(BF)
    near_q = near_sum(g_qkv.reshape(clip_count, d_rows, 3 * head_cols), "clip")
    back, gain1, shift1 = norm_backward(g_attin, normed1, inv1, norm_gains[1])
    grad1 = grad2 + back

    half0 = 0.5 * grad1
    g_bout0 = jnp.sum(half0, axis=0)
    half0_all = lax.all_gather(half0.astype(BF), "seq", axis=0, tiled=True)
    gpre0 = mm_nt(half0_all, got_out0) * swish_slope(pre0)
    gpre0_b = gpre0.astype(BF)
    g_bin0 = jnp.sum(gpre0, axis=0)
    gpre0_b, near_q = tie(gpre0_b, near_q)
    own_qkv = far_sum(near_q, "clip")
    g_out0 = mm_tn(hid0, half0_all).astype(BF)
    g_in0 = mm_tn(ffin0, gpre0_b).astype(BF)

    bin_full = jnp.zeros((clip_count, 2, seq_count, h_part), F32)
    bin_full = lax.dynamic_update_slice_in_dim(
        bin_full,
        jnp.stack([g_bin0, g_bin1]).reshape(2, clip_count, 1, h_part).transpose(1, 0, 2, 3),
        place,
        2,
    )
    sum_lines = jnp.concatenate(
        [
            jnp.stack([g_bout0, g_bout1]),
            g_affine,
            jnp.stack([gain1, gain2, gain3, gain4, shift1, shift2, shift3, shift4]),
            g_depth,
        ],
        axis=0,
    )
    n_lines = sum_lines.shape[0]
    sum_pack = jnp.concatenate(
        [
            sum_lines.reshape(n_lines, clip_count, d_rows).transpose(1, 0, 2),
            bin_full.reshape(clip_count, 2 * h_rows // d_rows, d_rows),
        ],
        axis=1,
    ).astype(BF)
    n_small = sum_pack.shape[1] * d_rows
    s_rows = pl.cdiv(n_small, width)
    sum_pack = jnp.pad(
        sum_pack.reshape(clip_count, n_small), ((0, 0), (0, s_rows * width - n_small))
    ).reshape(clip_count, s_rows, width)
    near0 = near_sum(
        jnp.concatenate(
            ff_pack(g_in0, g_out0) + [fit(sum_pack)],
            axis=1,
        ),
        "clip",
    )
    part = mm_nt(gpre0_b, got_in0).astype(BF)
    g_ffin = scatter_sum(part.reshape(seq_count, rows, width), "seq")
    g_ffin, near0, row_c, own_qkv = tie(g_ffin, near0, row_c, own_qkv)
    own_c = far_sum(near_sum(row_c, "clip"), "clip")

    own0 = far_sum(near0, "clip")
    back, gain0, shift0 = norm_backward(g_ffin, normed0, inv0, norm_gains[0])
    grad0 = grad1 + back
    slope_full = lax.dynamic_update_slice_in_dim(
        jnp.zeros((HEADS,), F32), jnp.stack(grad_slope), place * head_count, 0
    )
    last = jnp.concatenate(
        [gain0.reshape(clip_count, d_rows), shift0.reshape(clip_count, d_rows)], axis=1
    )
    slope_rows = jnp.zeros((clip_count, 2 * d_rows), F32).at[:, :HEADS].set(slope_full)
    last = jnp.stack([last, slope_rows], axis=1)
    last = jnp.broadcast_to(last[:, None], (clip_count, seq_count) + last.shape[1:])
    last = lax.all_to_all(
        last.reshape((groups,) + last.shape[2:]), ("clip", "seq"), 0, 0, tiled=True
    )
    last = jnp.sum(last, axis=0)
    slope_total = last[1, :HEADS]
    gain0_own = last[0, :d_rows]
    shift0_own = last[0, d_rows:]

    all0 = lax.all_gather(jnp.concatenate([own0, fit(own_qkv)], axis=0), "seq", axis=0)
    all0, own1, own_c = tie(all0, own1, own_c)
    as_rows = stack_cols(own_c)
    early = lax.all_gather(jnp.concatenate([own1] + [fit(c) for c in as_rows], axis=0), "seq", axis=0)
    all1 = early[:, : d_rows + h_part]
    all_c = early[:, d_rows + h_part :, :width].reshape(seq_count, len(as_rows), d_part, width)
    all_c = all_c.transpose(0, 2, 1, 3).reshape(d_rows, m_cols).astype(F32)
    all_small = all0[:, d_rows + h_part : d_rows + h_part + s_rows, :width]
    all_small = jnp.sum(all_small.astype(F32), axis=0)
    all_small = all_small.reshape(-1)[:n_small].reshape(n_small // d_rows, d_rows)
    all_qkv = all0[:, d_rows + h_part + s_rows :, : 3 * head_cols]

    def ff_grads(full):
        g_in = full[:, :d_rows, :sub].reshape(seq_count, d_rows, clip_count, h_part)
        g_in = g_in.transpose(1, 2, 0, 3).reshape(d_rows, hidden)
        g_out = full[:, d_rows : d_rows + h_part, :width].reshape(h_rows, width)
        return (g_in.astype(F32), g_out.astype(F32))

    o_in0, o_out0 = ff_grads(all0)
    o_in1, o_out1 = ff_grads(all1)
    o_convout = all_c[:, :width]
    o_attnout = all_c[:, width : 2 * width]
    o_convin = all_c[:, 2 * width :]
    o_attn = (
        all_qkv.reshape(seq_count, d_rows, 3, head_cols)
        .transpose(2, 1, 0, 3)
        .reshape(3, d_rows, width)
        .astype(F32)
    )
    o_bin = all_small[n_lines:].reshape(2, h_rows)
    o_gain = jnp.concatenate([gain0_own[None], all_small[4:8]], axis=0)
    o_shift = jnp.concatenate([shift0_own[None], all_small[8:12]], axis=0)
    return (
        final.astype(BF)[None],
        grad0[None],
        jnp.stack([o_in0, o_in1]),
        o_bin,
        jnp.stack([o_out0, o_out1]),
        all_small[0:2],
        o_attn,
        o_attnout,
        o_convin,
        all_small[12:n_lines],
        o_convout,
        all_small[2:4],
        o_gain,
        o_shift,
        slope_total,
    )


def solution(mesh):
    in_specs = (
        P("clip", "seq", None),
        P("clip"),
        P(None, "clip", None),
        P(None, "clip"),
        P(None, "clip", None),
        P(None, "clip"),
        P(None, "clip", None),
        P("clip", None),
        P("clip", None),
        P(None, "clip"),
        P("clip", None),
        P(None, "clip"),
        P(None, "clip"),
        P(None, "clip"),
        P(),
        P("clip", "seq", None),
    )
    out_specs = (
        P("clip", "seq", None),
        P("clip", "seq", None),
        P(None, "clip", None),
        P(None, "clip"),
        P(None, "clip", None),
        P(None, "clip"),
        P(None, "clip", None),
        P("clip", None),
        P("clip", None),
        P(None, "clip"),
        P("clip", None),
        P(None, "clip"),
        P(None, "clip"),
        P(None, "clip"),
        P(),
    )
    return jax.shard_map(
        on_device, mesh=mesh, in_specs=in_specs, out_specs=out_specs, check_vma=False
    )
```

```python
import jax
import jax.numpy as jnp
from jax import lax
from jax.experimental import pallas as pl
from jax.experimental.pallas import tpu as pltpu
from jax.sharding import PartitionSpec as P

HEADS = 8
KERNEL = 31
HEAD_DIM = 64


NORM_EPS = 1e-05
SCORE_SCALE = 0.125
BF = jnp.bfloat16
F32 = jnp.float32


def mm(a, b, dims):
    return lax.dot_general(a, b, (dims, ((), ())), preferred_element_type=F32)


def mm_nn(a, b):
    return mm(a, b, ((1,), (0,)))


def mm_nt(a, b):
    return mm(a, b, ((1,), (1,)))


def mm_tn(a, b):
    return mm(a, b, ((0,), (0,)))


def shift_pairs(count, step):
    return [(j, (j + step) % count) for j in range(count)]


def far_parts(block):
    count = lax.axis_size("clip")
    far = range(1, count // 2)
    return [block] + [lax.ppermute(block, "clip", shift_pairs(count, 2 * k)) for k in far]


def place_parts(parts, cuts):
    count = lax.axis_size("clip")
    place = lax.axis_index("clip")
    swap = [(j, j ^ 1) for j in range(count)]
    parts = parts + [lax.ppermute(part, "clip", swap) for part in parts]
    rows, dtype = parts[0].shape[0], parts[0].dtype

    def kernel(spot, *refs):
        for k in range(count):
            step = 2 * (k % (count // 2))
            source = lax.rem(spot[k // (count // 2)] + (count - step), count)
            for (start, size), out in zip(cuts, refs[count:]):
                out[source] = refs[k][:, start : start + size]

    vmem = pl.BlockSpec(memory_space=pltpu.VMEM)
    return pl.pallas_call(
        kernel,
        out_shape=[jax.ShapeDtypeStruct((count, rows, size), dtype) for _, size in cuts],
        in_specs=[pl.BlockSpec(memory_space=pltpu.SMEM)] + [vmem] * count,
        out_specs=[vmem] * len(cuts),
        name="place_blocks",
    )(jnp.stack([place, place ^ 1]).astype(jnp.int32), *parts)


def scatter_sum(blocks, axis):
    count = lax.axis_size(axis)
    place = lax.axis_index(axis)
    total = lax.dynamic_index_in_dim(blocks, place, 0, False).astype(F32)
    for k in range(1, count):
        piece = lax.dynamic_index_in_dim(blocks, (place + k) % count, 0, False)
        total = total + lax.ppermute(piece, axis, shift_pairs(count, k)).astype(F32)
    return total


def rows_to_cols(block):
    count = lax.axis_size("seq")
    place = lax.axis_index("seq")
    rows, cols = block.shape[0] // count, block.shape[1]
    mine = lax.dynamic_slice_in_dim(block, place * rows, rows, 0)
    full = jnp.zeros((rows, cols * count), block.dtype)
    full = lax.dynamic_update_slice_in_dim(full, mine, place * cols, 1)
    for k in range(1, count):
        piece = lax.dynamic_slice_in_dim(block, (place + k) % count * rows, rows, 0)
        piece = lax.ppermute(piece, "seq", shift_pairs(count, k))
        full = lax.dynamic_update_slice_in_dim(full, piece, (place - k) % count * cols, 1)
    return full


def cols_to_rows(block):
    count = lax.axis_size("seq")
    place = lax.axis_index("seq")
    rows, cols = block.shape[0], block.shape[1] // count
    mine = lax.dynamic_slice_in_dim(block, place * cols, cols, 1)
    full = jnp.zeros((rows * count, cols), block.dtype)
    full = lax.dynamic_update_slice_in_dim(full, mine, place * rows, 0)
    for k in range(1, count):
        piece = lax.dynamic_slice_in_dim(block, (place + k) % count * cols, cols, 1)
        piece = lax.ppermute(piece, "seq", shift_pairs(count, k))
        full = lax.dynamic_update_slice_in_dim(full, piece, (place - k) % count * rows, 0)
    return full


def near_sum(blocks, axis, dim=0):
    count = lax.axis_size(axis)
    low = lax.axis_index(axis) % 2
    shape = blocks.shape
    grid = blocks.reshape(shape[:dim] + (count // 2, 2) + shape[dim + 1 :])
    mine = lax.dynamic_index_in_dim(grid, low, dim + 1, False)
    other = lax.dynamic_index_in_dim(grid, 1 - low, dim + 1, False)
    other = lax.ppermute(other, axis, [(j, j ^ 1) for j in range(count)])
    return (mine.astype(F32) + other.astype(F32)).astype(BF)


def far_sum(both, axis, dim=0):
    count = lax.axis_size(axis)
    half = count // 2
    high = lax.axis_index(axis) // 2
    total = lax.dynamic_index_in_dim(both, high, dim, False).astype(F32)
    got = []
    for k in range(1, half):
        piece = lax.dynamic_index_in_dim(both, (high + k) % half, dim, False)
        got.append(lax.ppermute(piece, axis, shift_pairs(count, 2 * k)))
    for piece in got:
        total = total + piece.astype(F32)
    return total.astype(BF)


def owners(grad, rows, cols):
    return grad.reshape(lax.axis_size("clip"), lax.axis_size("seq"), rows, cols)


def tie(value, *others):
    return lax.optimization_barrier((value,) + others)


def total_all(rows):
    count = lax.axis_size("clip") * lax.axis_size("seq")
    spread = jnp.broadcast_to(rows[None], (count,) + rows.shape)
    return jnp.sum(lax.all_to_all(spread, ("clip", "seq"), 0, 0, tiled=True), axis=0)


def with_halo(block):
    count = lax.axis_size("seq")
    forward = [(i, i + 1) for i in range(count - 1)]
    backward = [(target, source) for source, target in forward]
    low = lax.ppermute(block[block.shape[0] - HALO :], "seq", forward)
    high = lax.ppermute(block[:HALO], "seq", backward)
    return (low, block, high)


def swish(values):
    return values * jax.nn.sigmoid(values)


def swish_slope(values):
    sigmoid_v = jax.nn.sigmoid(values)
    return sigmoid_v * (1.0 + values * (1.0 - sigmoid_v))


def norm_forward(resid, gain, shift):
    average = jnp.mean(resid, axis=-1, keepdims=True)
    centred = resid - average
    variance = jnp.mean(centred * centred, axis=-1, keepdims=True)
    inv_std = lax.rsqrt(variance + NORM_EPS)
    normed = centred * inv_std
    return (normed * gain + shift, normed, inv_std)


def norm_backward(cotangent, normed, inv_std, gain):
    scaled = cotangent * gain
    inner_sum = (
        scaled
        - jnp.mean(scaled, axis=-1, keepdims=True)
        - normed * jnp.mean(scaled * normed, axis=-1, keepdims=True)
    )
    return (inv_std * inner_sum, jnp.sum(cotangent * normed, axis=0), jnp.sum(cotangent, axis=0))


HALO = 16
LANES = 128


def load_padded(buf, low, block, high):
    rows = block.shape[0]
    buf[0:HALO, :] = low[...].astype(F32)
    buf[HALO : HALO + rows, :] = block[...].astype(F32)
    buf[HALO + rows : 2 * HALO + rows, :] = high[...].astype(F32)


def conv_kernel(low, block, high, mask, depth, conv, stats, buf):
    rows, width = block.shape
    load_padded(buf, low, block, high)
    keep = mask[...]

    @pl.loop(0, width // LANES)
    def _(step):
        cols = pl.ds(pl.multiple_of(step * LANES, LANES), LANES)
        total = jnp.zeros((rows, LANES), F32)
        for low_bits in range(8):
            shifted = buf[low_bits : low_bits + rows + 24, cols]
            for high_bits in range(4):
                tap = 8 * high_bits + low_bits - 1
                if 0 <= tap < KERNEL:
                    total = total + depth[tap : tap + 1, cols] * shifted[
                        8 * high_bits : 8 * high_bits + rows
                    ]
        conv[:, cols] = total
        kept = keep * total
        stats[0:1, cols] = jnp.sum(kept, axis=0, keepdims=True)
        stats[1:2, cols] = jnp.sum(kept * total, axis=0, keepdims=True)
        stats[2:3, cols] = jnp.broadcast_to(jnp.sum(keep, axis=0, keepdims=True), (1, LANES))


def depth_conv(low, block, high, mask, depth):
    rows, width = block.shape
    return pl.pallas_call(
        conv_kernel,
        out_shape=(
            jax.ShapeDtypeStruct((rows, width), F32),
            jax.ShapeDtypeStruct((3, width), F32),
        ),
        scratch_shapes=[pltpu.VMEM((rows + 2 * HALO, width), F32)],
        name="depth_conv",
    )(low, block, high, mask, depth)


def back_kernel(
    low, block, high, glow, gblock, ghigh, mask, linear, gate, depth, gmixed, gdepth, buf, gbuf
):
    rows, width = block.shape
    load_padded(buf, low, block, high)
    load_padded(gbuf, glow, gblock, ghigh)
    keep = mask[...]

    @pl.loop(0, width // LANES)
    def _(block_step):
        start = pl.multiple_of(block_step * LANES, LANES)
        cols = pl.ds(start, LANES)
        here = gblock[:, cols].astype(F32)
        total = jnp.zeros((rows, LANES), F32)
        for low_bits in range(8):
            shifted = buf[low_bits : low_bits + rows + 24, cols]
            gshifted = gbuf[low_bits : low_bits + rows + 24, cols]
            for high_bits in range(4):
                span = slice(8 * high_bits, 8 * high_bits + rows)
                step = 8 * high_bits + low_bits
                tap = step - 1
                if 0 <= tap < KERNEL:
                    gdepth[tap : tap + 1, cols] = jnp.sum(
                        here * shifted[span], axis=0, keepdims=True
                    )
                tap = KERNEL - step
                if 0 <= tap < KERNEL:
                    total = total + depth[tap : tap + 1, cols] * gshifted[span]
        total = keep * total
        open_v = gate[:, cols]
        first = total * open_v
        gmixed[:, cols] = first.astype(BF)
        gmixed[:, pl.ds(pl.multiple_of(width + start, LANES), LANES)] = (
            first * linear[:, cols] * (1.0 - open_v)
        ).astype(BF)


def depth_back(padded, grads, mask, linear, gate, depth):
    rows, width = linear.shape
    return pl.pallas_call(
        back_kernel,
        out_shape=(
            jax.ShapeDtypeStruct((rows, 2 * width), BF),
            jax.ShapeDtypeStruct((KERNEL, width), F32),
        ),
        scratch_shapes=[pltpu.VMEM((rows + 2 * HALO, width), F32)] * 2,
        name="depth_back",
    )(*padded, *grads, mask, linear, gate, depth)


def head_split(cols):
    return [cols[:, i : i + HEAD_DIM] for i in range(0, cols.shape[1], HEAD_DIM)]


def on_device(
    clips,
    lengths,
    ff_in,
    ff_in_bias,
    ff_out,
    ff_out_bias,
    attn_in,
    attn_out,
    conv_in,
    conv_depth,
    conv_out,
    bn_affine,
    norm_gain,
    norm_bias,
    slope,
    out_grad,
):
    clip_count = lax.axis_size("clip")
    seq_count = lax.axis_size("seq")
    place = lax.axis_index("seq")
    rows = clips.shape[1]
    tokens = rows * seq_count
    width = clips.shape[2]
    hidden = ff_in.shape[2]
    d_rows = ff_in.shape[1]
    h_rows = ff_out.shape[1]
    h_part = h_rows // seq_count
    d_part = d_rows // seq_count
    head_cols = width // seq_count
    head_count = HEADS // seq_count

    sub = clip_count * h_part
    ins = [w.reshape(d_rows, clip_count, seq_count, h_part) for w in (ff_in[0], ff_in[1])]
    ins = [lax.dynamic_index_in_dim(w, place, 2, False).reshape(d_rows, sub) for w in ins]
    outs = lax.dynamic_slice_in_dim(ff_out, place * h_part, h_part, 1)
    smalls = jnp.concatenate(
        [
            ff_out_bias,
            bn_affine,
            norm_gain,
            norm_bias,
            conv_depth,
            ff_in_bias.reshape(2 * h_rows // d_rows, d_rows),
        ],
        axis=0,
    )
    small_rows = smalls.shape[0]
    qkv = lax.dynamic_slice_in_dim(attn_in, place * head_cols, head_cols, 2)
    p_rows = max(d_rows, h_part)
    lanes = pl.cdiv(small_rows, LANES) * LANES

    def padded_to(block, cols):
        return jnp.pad(block, ((0, p_rows - block.shape[0]), (0, cols - block.shape[1])))

    first = jnp.concatenate(
        [padded_to(ins[0], sub), padded_to(outs[0], width), padded_to(smalls.T, lanes)]
        + [padded_to(qkv[i], head_cols) for i in range(3)],
        axis=1,
    )
    sizes = [sub, width, lanes, 3 * head_cols]
    cuts = [(sum(sizes[:i]), size) for i, size in enumerate(sizes)]
    late = jnp.concatenate(
        [padded_to(attn_out, width), padded_to(conv_in, conv_in.shape[1])]
        + [padded_to(conv_out, width), padded_to(ins[1], sub), padded_to(outs[1], width)],
        axis=1,
    )
    first = far_parts(first)
    first[1], late = tie(first[1], late)
    late = far_parts(late)
    got = place_parts(first, cuts)
    got_in0 = got[0][:, :d_rows].reshape(width, sub)
    got_out0 = got[1][:, :h_part].reshape(sub, width)
    got_small = got[2][:, :d_rows].reshape(width, lanes)[:, :small_rows]
    w_qkv = got[3][:, :d_rows].reshape(width, 3 * head_cols)

    lines = got_small.astype(F32).T
    n_vec = small_rows - 2 * h_rows // d_rows
    ffout_bias = lines[0:2]
    affine = lines[2:4]
    norm_gains = lines[4:9]
    shifts = lines[9:14]
    w_depth = lines[14:n_vec]
    bias_in = lines[n_vec:].reshape(2, h_rows // d_rows, clip_count, d_rows)
    bias_in = bias_in.transpose(0, 2, 1, 3).reshape(2, hidden)
    bias_in = bias_in.reshape(2, clip_count, seq_count, h_part)
    bias_in = lax.dynamic_index_in_dim(bias_in, place, 2, False).reshape(2, sub)

    length = lengths[0]
    positions = place * rows + jnp.arange(rows, dtype=jnp.int32)
    token_mask = (positions < length).astype(F32)[:, None]
    head_slope = lax.dynamic_slice_in_dim(slope, place * head_count, head_count, 0)

    clips_all = lax.all_gather(clips[0], "seq", axis=0, tiled=True)
    ffin0 = norm_forward(clips_all.astype(F32), norm_gains[0], shifts[0])[0].astype(BF)
    resid0 = clips[0].astype(F32)
    _, normed0, inv0 = norm_forward(resid0, norm_gains[0], shifts[0])
    pre0 = mm_nn(ffin0, got_in0) + bias_in[0]
    hid0 = swish(pre0).astype(BF)
    part = mm_nn(hid0, got_out0).astype(BF)
    ff_sum = scatter_sum(part.reshape(seq_count, rows, width), "seq")
    ff_sum, *late = tie(ff_sum, *late)
    resid1 = resid0 + 0.5 * (ff_sum + ffout_bias[0])
    c_cols = conv_in.shape[1]
    sizes = [width, c_cols, width, sub, width]
    cuts = [(sum(sizes[:i]), size) for i, size in enumerate(sizes)]
    got = place_parts(late, cuts)
    w_attnout, w_convin, w_convout = [w[:, :d_rows].reshape(width, -1) for w in got[:3]]
    got_in1 = got[3][:, :d_rows].reshape(width, sub)
    got_out1 = got[4][:, :h_part].reshape(sub, width)

    att_norm, normed1, inv1 = norm_forward(resid1, norm_gains[1], shifts[1])
    attin = lax.all_gather(att_norm.astype(BF), "seq", axis=0, tiled=True)
    qkv_all = mm_nn(attin, w_qkv).astype(BF)
    q_heads = head_split(qkv_all[:, :head_cols])
    k_heads = head_split(qkv_all[:, head_cols : 2 * head_cols])
    v_heads = head_split(qkv_all[:, 2 * head_cols :])
    spot = jnp.arange(tokens, dtype=jnp.int32)
    distance = jnp.log1p(jnp.abs(spot[:, None] - spot[None, :]).astype(F32))
    key_ok = (spot < length)[None, :]
    probs = []
    head_outs = []
    for h in range(head_count):
        scores = mm_nt(q_heads[h], k_heads[h]) * SCORE_SCALE - head_slope[h] * distance
        scores = jnp.where(key_ok, scores, -jnp.inf)
        highest = jnp.max(scores, axis=-1, keepdims=True)
        log_total = highest + jnp.log(jnp.sum(jnp.exp(scores - highest), axis=-1, keepdims=True))
        prob = jnp.exp(scores - log_total)
        probs.append(prob)
        head_outs.append(mm_nn(prob.astype(BF), v_heads[h]).astype(BF))
    head_out = jnp.concatenate(head_outs, axis=1)
    att_tok = rows_to_cols(head_out)
    resid2 = resid1 + mm_nn(att_tok, w_attnout)

    conv_norm, normed2, inv2 = norm_forward(resid2, norm_gains[2], shifts[2])
    convin = conv_norm.astype(BF)
    mixed = mm_nn(convin, w_convin)
    linear = mixed[:, :width]
    gate = jax.nn.sigmoid(mixed[:, width:])
    gated = (token_mask * linear * gate).astype(BF)
    padded = with_halo(gated)
    conv, stats = depth_conv(*padded, token_mask, w_depth)
    stats = total_all(stats)
    count = stats[2]
    average = stats[0] / count
    variance = stats[1] / count - average * average
    batch_inv = lax.rsqrt(variance + NORM_EPS)
    centred = conv - average
    bnormed = centred * batch_inv
    batch_out = bnormed * affine[0] + affine[1]
    activ = swish(batch_out).astype(BF)
    resid3 = resid2 + mm_nn(activ, w_convout)

    ff_norm, normed3, inv3 = norm_forward(resid3, norm_gains[3], shifts[3])
    ffin1 = lax.all_gather(ff_norm.astype(BF), "seq", axis=0, tiled=True)
    pre1 = mm_nn(ffin1, got_in1) + bias_in[1]
    hid1 = swish(pre1).astype(BF)
    part = mm_nn(hid1, got_out1).astype(BF)
    resid4 = resid3 + 0.5 * (
        scatter_sum(part.reshape(seq_count, rows, width), "seq") + ffout_bias[1]
    )
    final, normed4, inv4 = norm_forward(resid4, norm_gains[4], shifts[4])

    grad4, gain4, shift4 = norm_backward(out_grad[0].astype(F32), normed4, inv4, norm_gains[4])
    half1 = 0.5 * grad4
    g_bout1 = jnp.sum(half1, axis=0)
    half1_all = lax.all_gather(half1.astype(BF), "seq", axis=0, tiled=True)
    gpre1 = mm_nt(half1_all, got_out1) * swish_slope(pre1)
    gpre1_b = gpre1.astype(BF)
    g_bin1 = jnp.sum(gpre1, axis=0)
    part = mm_nt(gpre1_b, got_in1).astype(BF)
    g_ffin = scatter_sum(part.reshape(seq_count, rows, width), "seq")
    back, gain3, shift3 = norm_backward(g_ffin, normed3, inv3, norm_gains[3])
    grad3 = grad4 + back
    grad3_b = grad3.astype(BF)
    g_out1 = mm_tn(hid1, half1_all).astype(BF)
    g_in1 = mm_tn(ffin1, gpre1_b).astype(BF)
    g_convout = mm_tn(activ, grad3_b).astype(BF)
    groups = clip_count * seq_count
    wide = max(sub, width)

    def stack_cols(block):
        return [block[:, i : i + width] for i in range(0, block.shape[1], width)]

    def fit(block):
        spare = wide - block.shape[-1]
        return jnp.pad(block, [(0, 0)] * (block.ndim - 1) + [(0, spare)]) if spare else block

    def ff_pack(g_in, g_out):
        return [
            fit(g_in.reshape(clip_count, d_rows, sub)),
            fit(g_out.reshape(clip_count, h_part, width)),
        ]

    near1 = near_sum(jnp.concatenate(ff_pack(g_in1, g_out1), axis=1), "clip")

    gbn = mm_nt(grad3_b, w_convout) * swish_slope(batch_out)
    g_affine = jnp.stack([jnp.sum(gbn * bnormed, axis=0), jnp.sum(gbn, axis=0)])
    gcent = gbn * affine[0]
    sums = total_all(jnp.stack([jnp.sum(gcent, axis=0), jnp.sum(gcent * centred, axis=0)]))
    sums, near1 = tie(sums, near1)
    own1 = far_sum(near1, "clip")
    grad_var = -0.5 * batch_inv**3 * sums[1]
    grad_avg = -batch_inv * sums[0] - 2.0 * average * grad_var
    gconv = (
        gcent * batch_inv + token_mask * (grad_avg + 2.0 * grad_var * conv) / count
    ).astype(BF)
    gmixed, g_depth = depth_back(padded, with_halo(gconv), token_mask, linear, gate, w_depth)
    back, gain2, shift2 = norm_backward(mm_nt(gmixed, w_convin), normed2, inv2, norm_gains[2])
    grad2 = grad3 + back
    grad2_b = grad2.astype(BF)
    gatt = mm_nt(grad2_b, w_attnout).astype(BF)
    gatt_all = cols_to_rows(gatt)
    g_convin = mm_tn(convin, gmixed).astype(BF)
    g_attnout = mm_tn(att_tok, grad2_b).astype(BF)
    g_mixed = jnp.concatenate([g_convout, g_attnout, g_convin], axis=1)
    m_cols = g_mixed.shape[1]
    core_c = near_sum(owners(g_mixed, d_part, m_cols), "seq", 1)

    grad_q = []
    grad_k = []
    grad_v = []
    grad_slope = []
    for h, g_head in enumerate(head_split(gatt_all)):
        prob = probs[h]
        gprob = mm_nt(g_head, v_heads[h])
        inner = jnp.sum(prob * gprob, axis=-1, keepdims=True)
        gscore = prob * (gprob - inner)
        grad_slope.append(-jnp.sum(gscore * distance))
        gscore_b = gscore.astype(BF)
        grad_q.append((SCORE_SCALE * mm_nn(gscore_b, k_heads[h])).astype(BF))
        grad_k.append((SCORE_SCALE * mm_tn(gscore_b, q_heads[h])).astype(BF))
        grad_v.append(mm_tn(prob.astype(BF), g_head).astype(BF))
    gqkv = jnp.concatenate(grad_q + grad_k + grad_v, axis=1)
    gqkv, own1, core_c = tie(gqkv, own1, core_c)
    part = mm_nt(gqkv, w_qkv).astype(BF)
    g_attin = scatter_sum(part.reshape(seq_count, rows, width), "seq")
    g_qkv = mm_tn(attin, gqkv).astype(BF)
    near_q = near_sum(g_qkv.reshape(clip_count, d_rows, 3 * head_cols), "clip")
    back, gain1, shift1 = norm_backward(g_attin, normed1, inv1, norm_gains[1])
    grad1 = grad2 + back

    half0 = 0.5 * grad1
    g_bout0 = jnp.sum(half0, axis=0)
    half0_all = lax.all_gather(half0.astype(BF), "seq", axis=0, tiled=True)
    gpre0 = mm_nt(half0_all, got_out0) * swish_slope(pre0)
    gpre0_b = gpre0.astype(BF)
    g_bin0 = jnp.sum(gpre0, axis=0)
    gpre0_b, near_q = tie(gpre0_b, near_q)
    own_qkv = far_sum(near_q, "clip")
    g_out0 = mm_tn(hid0, half0_all).astype(BF)
    g_in0 = mm_tn(ffin0, gpre0_b).astype(BF)

    bin_full = jnp.zeros((clip_count, 2, seq_count, h_part), F32)
    bin_full = lax.dynamic_update_slice_in_dim(
        bin_full,
        jnp.stack([g_bin0, g_bin1]).reshape(2, clip_count, 1, h_part).transpose(1, 0, 2, 3),
        place,
        2,
    )
    sum_lines = jnp.concatenate(
        [
            jnp.stack([g_bout0, g_bout1]),
            g_affine,
            jnp.stack([gain1, gain2, gain3, gain4, shift1, shift2, shift3, shift4]),
            g_depth,
        ],
        axis=0,
    )
    n_lines = sum_lines.shape[0]
    sum_pack = jnp.concatenate(
        [
            sum_lines.reshape(n_lines, clip_count, d_rows).transpose(1, 0, 2),
            bin_full.reshape(clip_count, 2 * h_rows // d_rows, d_rows),
        ],
        axis=1,
    ).astype(BF)
    n_small = sum_pack.shape[1] * d_rows
    s_rows = pl.cdiv(n_small, width)
    sum_pack = jnp.pad(
        sum_pack.reshape(clip_count, n_small), ((0, 0), (0, s_rows * width - n_small))
    ).reshape(clip_count, s_rows, width)
    near0 = near_sum(
        jnp.concatenate(
            ff_pack(g_in0, g_out0) + [fit(sum_pack)],
            axis=1,
        ),
        "clip",
    )
    part = mm_nt(gpre0_b, got_in0).astype(BF)
    g_ffin = scatter_sum(part.reshape(seq_count, rows, width), "seq")
    g_ffin, near0, core_c, own_qkv = tie(g_ffin, near0, core_c, own_qkv)
    row_c = far_sum(core_c, "seq", 1)
    own_c = far_sum(near_sum(row_c, "clip"), "clip")

    own0 = far_sum(near0, "clip")
    back, gain0, shift0 = norm_backward(g_ffin, normed0, inv0, norm_gains[0])
    grad0 = grad1 + back
    slope_full = lax.dynamic_update_slice_in_dim(
        jnp.zeros((HEADS,), F32), jnp.stack(grad_slope), place * head_count, 0
    )
    last = jnp.concatenate(
        [gain0.reshape(clip_count, d_rows), shift0.reshape(clip_count, d_rows)], axis=1
    )
    slope_rows = jnp.zeros((clip_count, 2 * d_rows), F32).at[:, :HEADS].set(slope_full)
    last = jnp.stack([last, slope_rows], axis=1)
    last = jnp.broadcast_to(last[:, None], (clip_count, seq_count) + last.shape[1:])
    last = lax.all_to_all(
        last.reshape((groups,) + last.shape[2:]), ("clip", "seq"), 0, 0, tiled=True
    )
    last = jnp.sum(last, axis=0)
    slope_total = last[1, :HEADS]
    gain0_own = last[0, :d_rows]
    shift0_own = last[0, d_rows:]

    all0 = lax.all_gather(jnp.concatenate([own0, fit(own_qkv)], axis=0), "seq", axis=0)
    all0, own1, own_c = tie(all0, own1, own_c)
    as_rows = stack_cols(own_c)
    early = lax.all_gather(jnp.concatenate([own1] + [fit(c) for c in as_rows], axis=0), "seq", axis=0)
    all1 = early[:, : d_rows + h_part]
    all_c = early[:, d_rows + h_part :, :width].reshape(seq_count, len(as_rows), d_part, width)
    all_c = all_c.transpose(0, 2, 1, 3).reshape(d_rows, m_cols).astype(F32)
    all_small = all0[:, d_rows + h_part : d_rows + h_part + s_rows, :width]
    all_small = jnp.sum(all_small.astype(F32), axis=0)
    all_small = all_small.reshape(-1)[:n_small].reshape(n_small // d_rows, d_rows)
    all_qkv = all0[:, d_rows + h_part + s_rows :, : 3 * head_cols]

    def ff_grads(full):
        g_in = full[:, :d_rows, :sub].reshape(seq_count, d_rows, clip_count, h_part)
        g_in = g_in.transpose(1, 2, 0, 3).reshape(d_rows, hidden)
        g_out = full[:, d_rows : d_rows + h_part, :width].reshape(h_rows, width)
        return (g_in.astype(F32), g_out.astype(F32))

    o_in0, o_out0 = ff_grads(all0)
    o_in1, o_out1 = ff_grads(all1)
    o_convout = all_c[:, :width]
    o_attnout = all_c[:, width : 2 * width]
    o_convin = all_c[:, 2 * width :]
    o_attn = (
        all_qkv.reshape(seq_count, d_rows, 3, head_cols)
        .transpose(2, 1, 0, 3)
        .reshape(3, d_rows, width)
        .astype(F32)
    )
    o_bin = all_small[n_lines:].reshape(2, h_rows)
    o_gain = jnp.concatenate([gain0_own[None], all_small[4:8]], axis=0)
    o_shift = jnp.concatenate([shift0_own[None], all_small[8:12]], axis=0)
    return (
        final.astype(BF)[None],
        grad0[None],
        jnp.stack([o_in0, o_in1]),
        o_bin,
        jnp.stack([o_out0, o_out1]),
        all_small[0:2],
        o_attn,
        o_attnout,
        o_convin,
        all_small[12:n_lines],
        o_convout,
        all_small[2:4],
        o_gain,
        o_shift,
        slope_total,
    )


def solution(mesh):
    in_specs = (
        P("clip", "seq", None),
        P("clip"),
        P(None, "clip", None),
        P(None, "clip"),
        P(None, "clip", None),
        P(None, "clip"),
        P(None, "clip", None),
        P("clip", None),
        P("clip", None),
        P(None, "clip"),
        P("clip", None),
        P(None, "clip"),
        P(None, "clip"),
        P(None, "clip"),
        P(),
        P("clip", "seq", None),
    )
    out_specs = (
        P("clip", "seq", None),
        P("clip", "seq", None),
        P(None, "clip", None),
        P(None, "clip"),
        P(None, "clip", None),
        P(None, "clip"),
        P(None, "clip", None),
        P("clip", None),
        P("clip", None),
        P(None, "clip"),
        P("clip", None),
        P(None, "clip"),
        P(None, "clip"),
        P(None, "clip"),
        P(),
    )
    return jax.shard_map(
        on_device, mesh=mesh, in_specs=in_specs, out_specs=out_specs, check_vma=False
    )
```
